256 devices in a mesh: ctx: 32 (over y, x, core), ep: 8 (over z).
Axes of the slice: x: 4, y: 4, z: 8, core: 2. Of those that a mesh axis runs over, the one named last changes fastest.
Arguments:
- out_grad: bfloat16 [8192, 2048], P('ctx'), may hold values from -12 to 12
- gate_values: bfloat16 [8192, 8], P('ctx'), may hold values from 0.049804688 to 0.3984375
- expert_ids: int32 [8192, 8], P('ctx'), may hold values from 0 to 63, all different within a row; in each aligned block of 256 rows (0 to 255, 256 to 511, ...) at most 48 rows name the same one
- segment_ids: int32 [8192], P('ctx'), may hold values from 0 to 15, never falling along the last dimension, each value on 1 to 1793 neighbouring positions
- gate_pre: bfloat16 [256, 32, 48, 256], P(('ctx', 'ep')), may hold values from -6 to 6
- up_pre: bfloat16 [256, 32, 48, 256], P(('ctx', 'ep')), may hold values from -6 to 6
- w_gate: bfloat16 [256, 2048, 256], P(('ctx', 'ep')), may hold values from -0.125 to 0.125
- w_up: bfloat16 [256, 2048, 256], P(('ctx', 'ep')), may hold values from -0.125 to 0.125
- w_down: bfloat16 [256, 256, 2048], P(('ctx', 'ep')), may hold values from -0.1875 to 0.1875
- queries: bfloat16 [8192, 2048], P('ctx', 'ep'), may hold values from -0.015625 to 0.015625
- keys: bfloat16 [8192, 2048], P('ctx', 'ep'), may hold values from -0.015625 to 0.015625
- values: bfloat16 [8192, 2048], P('ctx', 'ep'), may hold values from -6 to 6
Outputs:
- query_grad: bfloat16 [8192, 2048], P('ctx', 'ep')
- key_grad: bfloat16 [8192, 2048], P('ctx', 'ep')
- value_grad: bfloat16 [8192, 2048], P('ctx', 'ep')
- down_grad: float32 [256, 256, 2048], P(('ctx', 'ep'))
The draws below stay inside these ranges and needn't reach their ends.
Inputs may be any that keep to these rules, and one draw needn't show every extreme that they name: `expert_ids`: each token names 8 different experts. Among the 256 tokens of one context shard at most 48 name the same expert, and in every draw some shard has exactly 48 tokens that name one expert. `segment_ids`: document numbers never fall along the tokens; a document has 1 to 1793 tokens and one has exactly 1793, so that no document covers more than eight context shards of 256 tokens.
All inputs are finite; a program needn't handle non-finite values.
Results may differ from the reference program's by a relative error of at most 0.008.
Values may be sent and summed in bfloat16 or wider, within the bound.
A program may use at most 128 MiB of HBM per device.

```python
import math
import jax
import jax.numpy as jnp
import numpy as np
from jax import lax

D = 2048
HEADS = 16
HEAD_DIM = 128
FF = 1024
TOP = 8
TOK_DEV = 256
EXPERTS = 64
HSPLIT = 4
FFP = 256
MOST = 48
TOKENS = 8192
DOC_MOST = 1793
DOCS = 16
N_CTX = 32


def shard_levels(key, shape, cuts, smallest, high):
    loudness, own = 1.0, jax.random.fold_in(key, 6)
    for dim, blocks in cuts:
        steps = jnp.exp(jax.random.uniform(jax.random.fold_in(own, dim), (blocks,), jnp.float32, smallest / len(cuts), high / len(cuts)))
        loudness = loudness * jnp.repeat(steps, shape[dim] // blocks).reshape([-1 if axis == dim else 1 for axis in range(len(shape))])
    return loudness


def profile(number_of, total, bound, slope):
    weights = [(1 << 20) // math.isqrt(grade ** slope) + 1 for grade in range(2, number_of + 1)]
    spare, given = total - bound - (number_of - 1), [1] * (number_of - 1)
    while spare > 0:
        free = [i for i in range(number_of - 1) if given[i] < bound]
        pool, left = sum([weights[i] for i in free]), spare
        for i in free:
            extra = min(bound - given[i], max(1, left * weights[i] // pool), spare)
            given[i] = given[i] + extra
            spare = spare - extra
    return np.array([bound] + given)


def uneven(rng, amount, total, limit, slope):
    if amount == 2:
        one = jax.random.randint(rng, (), max(1, total - limit), min(limit, total - 1) + 1)
        return jnp.stack([one, total - one])
    sizes = jnp.asarray(profile(amount, total, limit, slope), jnp.int32)
    twos = (amount - 1) // 2
    donor, sink = sizes[1:1 + 2 * twos:2], sizes[2:2 + 2 * twos:2]
    room = jnp.minimum(donor - 1, limit - sink)
    moved = jax.random.randint(jax.random.fold_in(rng, 1), (twos,), 0, 1 << 20) % (room + 1)
    sizes = sizes.at[1:1 + 2 * twos:2].set(donor - moved).at[2:2 + 2 * twos:2].set(sink + moved)
    return sizes[jax.random.permutation(jax.random.fold_in(rng, 2), amount)]


def routed_block(stream_key, own, number, rows, count, top, bound, skew):
    sequence = jax.random.permutation(stream_key, count)
    packed, common = portions_of(count, rows * top, bound, skew, True), portions_of(count, rows * top, bound, skew, False)
    places = jnp.arange(count)

    def named(sizes, turn):
        used = int((sizes > 0).sum())
        fixed = max(1, used // 4)
        moved = fixed + (places - fixed + turn * (used - fixed)) % max(1, count - fixed)
        return jnp.zeros((count,), jnp.int32).at[sequence[jnp.where(places < fixed, places, moved)]].set(jnp.asarray(sizes, jnp.int32))

    sizes = jnp.where(number % 4 == 0, named(packed, number // 4), named(common, number - number // 4 - 1))
    mixed = jax.random.permutation(jax.random.fold_in(own, 3), count)
    donor, taker = mixed[0:count // 2 * 2:2], mixed[1:count // 2 * 2:2]
    room = jnp.minimum(sizes[donor] - 1, bound - sizes[taker]) // 2
    room = jnp.where((donor == sequence[0]) | (taker == sequence[0]) | (sizes[taker] == 0), 0, jnp.maximum(room, 0))
    moved = jax.random.randint(jax.random.fold_in(own, 4), (count // 2,), 0, 1 << 20) % (room + 1)
    sizes = sizes.at[donor].add(-moved).at[taker].add(moved)
    items = jnp.searchsorted(jnp.cumsum(sizes), jnp.arange(rows * top), side="right").astype(jnp.int32)
    listing = items.reshape(top, rows).T
    listing = listing[jax.random.permutation(jax.random.fold_in(own, 1), rows)]
    turn = jax.random.randint(jax.random.fold_in(own, 2), (rows, 1), 0, top)
    return jnp.take_along_axis(listing, (jnp.arange(top)[None, :] + turn) % top, axis=1)


def portions_of(number_of, total, limit, lean, full):
    loads = [(1 << 20) // math.isqrt(rank ** lean) + 1 for rank in range(1, number_of + 1)]
    largest = limit if full else min(limit, max(-(-total // number_of), total * loads[0] // sum(loads)))
    least = 1 if total - largest >= number_of - 1 else 0
    given, surplus = [largest] + [least] * (number_of - 1), total - largest - least * (number_of - 1)
    while surplus > 0:
        movable = [i for i in range(1, number_of) if given[i] < largest] or [i for i in range(1, number_of) if given[i] < limit]
        whole, budget = sum([loads[i] for i in movable]), surplus
        for i in movable:
            more = min(limit - given[i], max(1, budget * loads[i] // whole), surplus)
            given[i] = given[i] + more
            surplus = surplus - more
    return np.array(given)


def scatter_about(rng, shape, deviation, limit, cuts=(), held_as=jnp.bfloat16):
    factor_of = shard_levels(rng, shape, cuts, -0.22, 0.18) if cuts else 1.0
    values = jax.random.normal(rng, shape, jnp.float32) * deviation * factor_of
    return jnp.minimum(jnp.maximum(values, -limit), limit).astype(held_as)


def setup_inputs(seed: int = 0) -> dict:
    key_of = jax.random.split(jax.random.key(seed), 13)
    out_grad = scatter_about(key_of[0], (TOKENS, D), 2.0, 12.0, ((0, 32),))
    gate_values = jnp.clip(0.049804688 + 0.3486328 * jax.random.uniform(key_of[1], (TOKENS, TOP), jnp.float32) ** shard_levels(key_of[1], (TOKENS, TOP), ((0, 32),), -0.2, 0.2), 0.049804688, 0.3984375).astype(jnp.bfloat16)
    expert_ids_keys = jax.random.split(jax.random.fold_in(key_of[2], 1), TOKENS // TOK_DEV)
    expert_ids_turns = jax.random.permutation(jax.random.fold_in(key_of[2], 3), TOKENS // TOK_DEV)
    expert_ids = jax.vmap(lambda own, number: routed_block(jax.random.fold_in(key_of[2], 2), own, number, TOK_DEV, EXPERTS, TOP, MOST, 2))(expert_ids_keys, expert_ids_turns).reshape((TOKENS, TOP))
    segment_ids = jnp.searchsorted(jnp.cumsum(uneven(key_of[3], DOCS, TOKENS, DOC_MOST, 2)), jnp.arange(TOKENS), side="right").astype(jnp.int32)
    gate_pre = scatter_about(key_of[4], (EXPERTS * HSPLIT, N_CTX, MOST, FFP), 1.0, 6.0, ((0, 256),))
    up_pre = scatter_about(key_of[5], (EXPERTS * HSPLIT, N_CTX, MOST, FFP), 1.0, 6.0, ((0, 256),))
    w_gate = scatter_about(key_of[6], (EXPERTS * HSPLIT, D, FFP), D ** -0.5, 0.125, ((0, 256),))
    w_up = scatter_about(key_of[7], (EXPERTS * HSPLIT, D, FFP), D ** -0.5, 0.125, ((0, 256),))
    w_down = scatter_about(key_of[8], (EXPERTS * HSPLIT, FFP, D), FF ** -0.5, 0.1875, ((0, 256),))
    queries = scatter_about(key_of[9], (TOKENS, D), (4 * HEAD_DIM * TOK_DEV) ** -0.5, 0.015625, ((0, 32), (1, 8)))
    keys = scatter_about(key_of[10], (TOKENS, D), (4 * HEAD_DIM * TOK_DEV) ** -0.5, 0.015625, ((0, 32), (1, 8)))
    values = scatter_about(key_of[11], (TOKENS, D), 1.0, 6.0, ((0, 32), (1, 8)))
    return {"out_grad": out_grad, "gate_values": gate_values, "expert_ids": expert_ids, "segment_ids": segment_ids, "gate_pre": gate_pre, "up_pre": up_pre, "w_gate": w_gate, "w_up": w_up, "w_down": w_down, "queries": queries, "keys": keys, "values": values}


HIGHEST = lax.Precision.HIGHEST


def assignment_ranks(expert_ids):
    shards = expert_ids.reshape(N_CTX, TOK_DEV * TOP)
    labels = jnp.arange(EXPERTS, dtype=jnp.int32)

    def count_before(assignment_row):
        onehot = (assignment_row[:, None] == labels[None, :]).astype(jnp.int32)
        before = jnp.cumsum(onehot, axis=0) - onehot
        return jnp.sum(before * onehot, axis=1).astype(jnp.int32)

    return lax.map(count_before, shards).reshape(TOKENS * TOP)


def expert_rows(cotangent, pre_gate, pre_up, gate_matrix, up_matrix, down_matrix):
    down_part = lax.dot_general(cotangent, down_matrix, (((1,), (1,)), ((), ())), preferred_element_type=jnp.float32)
    gate_value = pre_gate.astype(jnp.float32)
    up_value = pre_up.astype(jnp.float32)
    sigmoid_gate = jax.nn.sigmoid(gate_value)
    hidden = (gate_value * sigmoid_gate * up_value).astype(jnp.bfloat16)
    down_grad = lax.dot_general(hidden, cotangent, (((0,), (0,)), ((), ())), preferred_element_type=jnp.float32)
    gate_delta = (down_part * up_value * sigmoid_gate * (1.0 + gate_value * (1.0 - sigmoid_gate))).astype(jnp.bfloat16)
    up_delta = (down_part * gate_value * sigmoid_gate).astype(jnp.bfloat16)
    input_part = lax.dot_general(gate_delta, gate_matrix, (((1,), (1,)), ((), ())), preferred_element_type=jnp.float32)
    input_part = input_part + lax.dot_general(up_delta, up_matrix, (((1,), (1,)), ((), ())), preferred_element_type=jnp.float32)
    return input_part.astype(jnp.bfloat16), down_grad


def within_block(query3, key3, value3, cot3, segment):
    positions = jnp.arange(segment.shape[0], dtype=jnp.int32)
    allowed = ((positions[:, None] >= positions[None, :]) & (segment[:, None] == segment[None, :])).astype(jnp.float32)
    query32 = query3.astype(jnp.float32)
    key32 = key3.astype(jnp.float32)
    value32 = value3.astype(jnp.float32)
    cot32 = cot3.astype(jnp.float32)
    cot_value = jnp.einsum("the,she->hts", cot32, value32, precision=HIGHEST) * allowed[None]
    query_key = jnp.einsum("the,she->hts", query32, key32, precision=HIGHEST) * allowed[None]
    query_grad = jnp.einsum("hts,she->the", cot_value, key32, precision=HIGHEST)
    key_grad = jnp.einsum("hts,the->she", cot_value, query32, precision=HIGHEST)
    value_grad = jnp.einsum("hts,the->she", query_key, cot32, precision=HIGHEST)
    return query_grad, key_grad, value_grad


def end_states(query3, key3, value3, cot3, segment):
    last_mask = (segment == segment[-1]).astype(jnp.float32)[:, None, None]
    first_mask = (segment == segment[0]).astype(jnp.float32)[:, None, None]
    forward_state = jnp.einsum("the,thf->hef", key3.astype(jnp.float32) * last_mask, value3.astype(jnp.float32), precision=HIGHEST)
    backward_state = jnp.einsum("the,thf->hef", query3.astype(jnp.float32) * first_mask, cot3.astype(jnp.float32), precision=HIGHEST)
    return forward_state, backward_state


def reference(out_grad, gate_values, expert_ids, segment_ids, gate_pre, up_pre, w_gate, w_up, w_down, queries, keys, values):
    flat_ids = expert_ids.reshape(TOKENS * TOP)
    slot_rank = assignment_ranks(expert_ids)
    token_of = (jnp.arange(TOKENS * TOP, dtype=jnp.int32) // TOP).astype(jnp.int32)
    shard_of = (token_of // TOK_DEV).astype(jnp.int32)
    flat_gates = gate_values.reshape(TOKENS * TOP)
    padded = jnp.concatenate([out_grad, jnp.zeros((1, D), out_grad.dtype)], axis=0)
    dump_slot = N_CTX * MOST

    def per_expert(y_grad, expert):
        position = jnp.where(flat_ids == expert, shard_of * MOST + slot_rank, dump_slot).astype(jnp.int32)
        slot_token = jnp.full((dump_slot,), TOKENS, jnp.int32).at[position].set(token_of, mode="drop")
        slot_gate = jnp.zeros((dump_slot,), gate_values.dtype).at[position].set(flat_gates, mode="drop")
        row_block = jnp.take(padded, slot_token, axis=0)
        cotangent = (slot_gate[:, None].astype(jnp.float32) * row_block.astype(jnp.float32)).astype(jnp.bfloat16)
        grads = []
        for hidden_part in range(HSPLIT):
            weight_row = (expert * HSPLIT + hidden_part).astype(jnp.int32)
            pre_gate = lax.dynamic_index_in_dim(gate_pre, weight_row, 0, keepdims=False).reshape(dump_slot, FFP)
            pre_up = lax.dynamic_index_in_dim(up_pre, weight_row, 0, keepdims=False).reshape(dump_slot, FFP)
            gate_matrix = lax.dynamic_index_in_dim(w_gate, weight_row, 0, keepdims=False)
            up_matrix = lax.dynamic_index_in_dim(w_up, weight_row, 0, keepdims=False)
            down_matrix = lax.dynamic_index_in_dim(w_down, weight_row, 0, keepdims=False)
            input_part, down_part_grad = expert_rows(cotangent, pre_gate, pre_up, gate_matrix, up_matrix, down_matrix)
            y_grad = y_grad.at[slot_token].add(input_part.astype(jnp.float32), mode="drop")
            grads.append(down_part_grad)
        return y_grad, jnp.stack(grads)

    y_grad, down_grads = lax.scan(per_expert, jnp.zeros((TOKENS, D), jnp.float32), jnp.arange(EXPERTS, dtype=jnp.int32))
    down_grad = down_grads.reshape(EXPERTS * HSPLIT, FFP, D)

    head_cot = y_grad.astype(jnp.bfloat16)
    block_shape = (N_CTX, TOK_DEV, HEADS, HEAD_DIM)
    seg_blocks = segment_ids.reshape(N_CTX, TOK_DEV)
    blocks = (queries.reshape(block_shape), keys.reshape(block_shape), values.reshape(block_shape), head_cot.reshape(block_shape), seg_blocks)

    def block_work(block):
        query3, key3, value3, cot3, segment = block
        inner = within_block(query3, key3, value3, cot3, segment)
        states = end_states(query3, key3, value3, cot3, segment)
        return inner + states

    inner_query, inner_key, inner_value, forward_states, backward_states = lax.map(block_work, blocks)
    firsts = seg_blocks[:, 0]
    lasts = seg_blocks[:, -1]
    empty_state = jnp.zeros((HEADS, HEAD_DIM, HEAD_DIM), jnp.float32)

    def forward_step(carried, item):
        state_sum, last_doc = carried
        local_state, first_doc, final_doc = item
        kept = jnp.where(final_doc == last_doc, state_sum, jnp.zeros_like(state_sum))
        return (local_state + kept, final_doc), (state_sum, last_doc)

    def backward_step(carried, item):
        back_sum, next_doc = carried
        local_state, first_doc, final_doc = item
        kept = jnp.where(first_doc == next_doc, back_sum, jnp.zeros_like(back_sum))
        return (local_state + kept, first_doc), (back_sum, next_doc)

    final_carry, (state_in, doc_in) = lax.scan(forward_step, (empty_state, jnp.int32(-1)), (forward_states, firsts, lasts))
    final_back, (back_in, doc_back) = lax.scan(backward_step, (empty_state, jnp.int32(-1)), (backward_states, firsts, lasts), reverse=True)

    def cross_work(block):
        key3, value3, cot3, segment, state_sum, doc_before, back_sum, doc_after = block
        before_mask = (segment == doc_before).astype(jnp.float32)[:, None, None]
        after_mask = (segment == doc_after).astype(jnp.float32)[:, None, None]
        query_part = jnp.einsum("thf,hef->the", cot3.astype(jnp.float32), state_sum, precision=HIGHEST) * before_mask
        key_part = jnp.einsum("thf,hef->the", value3.astype(jnp.float32), back_sum, precision=HIGHEST) * after_mask
        value_part = jnp.einsum("the,hef->thf", key3.astype(jnp.float32), back_sum, precision=HIGHEST) * after_mask
        return query_part, key_part, value_part

    outer_query, outer_key, outer_value = lax.map(cross_work, (blocks[1], blocks[2], blocks[3], seg_blocks, state_in, doc_in, back_in, doc_back))
    query_grad = (inner_query + outer_query).astype(jnp.bfloat16).reshape(TOKENS, D)
    key_grad = (inner_key + outer_key).astype(jnp.bfloat16).reshape(TOKENS, D)
    value_grad = (inner_value + outer_value).astype(jnp.bfloat16).reshape(TOKENS, D)
    return (query_grad, key_grad, value_grad, down_grad)
```

```python
import jax
import jax.numpy as jnp
from jax import lax
from jax.sharding import PartitionSpec as P

HEAD_DIM = 128


def dot(a, b, dims, batch=((), ())):
    return lax.dot_general(a, b, (dims, batch), preferred_element_type=jnp.float32)


def dispatch_matrix(gate_values, expert_ids, parity, owners, slot_count):
    tokens, top_count = expert_ids.shape
    experts = 2 * jnp.arange(owners, dtype=jnp.int32) + parity
    hit = expert_ids.T[:, None, :] == experts[None, :, None]
    named = jnp.any(hit, axis=0)
    gate = jnp.sum(jnp.where(hit, gate_values.T.astype(jnp.float32)[:, None, :], 0.0), axis=0)
    places = jnp.arange(tokens, dtype=jnp.int32)
    earlier = (places[:, None] < places[None, :]).astype(jnp.bfloat16)
    before = dot(named.astype(jnp.bfloat16), earlier, ((1,), (0,)))
    rank = jnp.where(named, before, -1.0)
    slots = jnp.arange(slot_count, dtype=jnp.int32).astype(jnp.float32)
    seated = rank[:, None, :] == slots[None, :, None]
    return seated.astype(jnp.bfloat16), jnp.where(seated, gate[:, None, :], 0.0).astype(jnp.bfloat16)


def expert_rows(cotangent, pre_gate, pre_up, gate_matrix, up_matrix, down_matrix):
    down_part = dot(cotangent, down_matrix, ((1,), (1,)))
    gate_value = pre_gate.astype(jnp.float32)
    up_value = pre_up.astype(jnp.float32)
    sigmoid_gate = jax.nn.sigmoid(gate_value)
    hidden = (gate_value * sigmoid_gate * up_value).astype(jnp.bfloat16)
    down_grad = dot(hidden, cotangent, ((0,), (0,)))
    gate_delta = (
        down_part * up_value * sigmoid_gate * (1.0 + gate_value * (1.0 - sigmoid_gate))
    ).astype(jnp.bfloat16)
    up_delta = (down_part * gate_value * sigmoid_gate).astype(jnp.bfloat16)
    input_part = dot(gate_delta, gate_matrix, ((1,), (1,))) + dot(up_delta, up_matrix, ((1,), (1,)))
    return input_part.astype(jnp.bfloat16), down_grad


def local(
    out_grad,
    gate_values,
    expert_ids,
    segment_ids,
    gate_pre,
    up_pre,
    w_gate,
    w_up,
    w_down,
    queries,
    keys,
    values,
):
    owners = lax.axis_size("ctx")
    groups = lax.axis_size("ep")
    here = lax.axis_index("ctx")
    parity = lax.axis_index("ep") // (groups // 2)
    tokens, width = out_grad.shape
    slot_count = gate_pre.shape[2]
    rows = owners * slot_count
    bf16 = jnp.bfloat16

    heads = queries.shape[1] // HEAD_DIM
    shape = (tokens, heads, HEAD_DIM)
    query3, key3, value3 = (a.reshape(shape).transpose(1, 0, 2) for a in (queries, keys, values))
    first_doc = (segment_ids == segment_ids[0]).astype(bf16)
    last_doc = (segment_ids == segment_ids[-1]).astype(bf16)
    ends = lax.all_gather(jnp.stack([segment_ids[0], segment_ids[-1]]), "ctx")
    order = jnp.arange(owners, dtype=jnp.int32)
    from_before = ((ends[:, 1] == segment_ids[0]) & (order < here)).astype(jnp.float32)
    from_after = ((ends[:, 0] == segment_ids[-1]) & (order > here)).astype(jnp.float32)
    per_head = ((0,), (0,))
    forward = dot(key3 * last_doc[None, :, None], value3, ((1,), (1,)), per_head)
    forwards = lax.all_gather(forward.astype(bf16), "ctx").astype(jnp.float32)
    state_in = jnp.sum(forwards * from_before[:, None, None, None], axis=0).astype(bf16)

    seated, weighted = dispatch_matrix(gate_values, expert_ids, parity, owners, slot_count)
    send = dot(weighted.reshape(rows, tokens), out_grad, ((1,), (0,))).astype(bf16)
    cotangent = lax.all_to_all(send, "ctx", split_axis=0, concat_axis=0, tiled=True)
    input_part, down_grad = expert_rows(
        cotangent,
        gate_pre[0].reshape(rows, -1),
        up_pre[0].reshape(rows, -1),
        w_gate[0],
        w_up[0],
        w_down[0],
    )
    returned = lax.all_to_all(input_part, "ctx", split_axis=0, concat_axis=0, tiled=True)
    token_sum = dot(seated.reshape(rows, tokens), returned, ((0,), (0,))).astype(bf16)
    parts = lax.all_to_all(token_sum, "ep", split_axis=1, concat_axis=0, tiled=True)
    head_cot = jnp.sum(parts.reshape(groups, tokens, -1).astype(jnp.float32), axis=0).astype(bf16)
    cot3 = head_cot.reshape(shape).transpose(1, 0, 2)

    backward = dot(query3 * first_doc[None, :, None], cot3, ((1,), (1,)), per_head)
    backwards = lax.all_gather(backward.astype(bf16), "ctx").astype(jnp.float32)
    back_in = jnp.sum(backwards * from_after[:, None, None, None], axis=0).astype(bf16)

    places = jnp.arange(tokens, dtype=jnp.int32)
    allowed = (places[:, None] >= places[None, :]) & (segment_ids[:, None] == segment_ids[None, :])
    cot_value = jnp.where(allowed[None], dot(cot3, value3, ((2,), (2,)), per_head), 0.0).astype(bf16)
    query_key = jnp.where(allowed[None], dot(query3, key3, ((2,), (2,)), per_head), 0.0).astype(bf16)
    query_grad = dot(cot_value, key3, ((2,), (1,)), per_head)
    key_grad = dot(cot_value, query3, ((1,), (1,)), per_head)
    value_grad = dot(query_key, cot3, ((1,), (1,)), per_head)
    query_grad += dot(cot3 * first_doc[None, :, None], state_in, ((2,), (2,)), per_head)
    key_grad += dot(value3 * last_doc[None, :, None], back_in, ((2,), (2,)), per_head)
    value_grad += dot(key3 * last_doc[None, :, None], back_in, ((2,), (1,)), per_head)

    def flat(a):
        return a.astype(bf16).transpose(1, 0, 2).reshape(tokens, -1)

    return flat(query_grad), flat(key_grad), flat(value_grad), down_grad[None]


def solution(mesh):
    row, col = P("ctx", None), P("ctx", "ep")
    both = ("ctx", "ep")
    pre, weight = P(both, None, None, None), P(both, None, None)
    return jax.shard_map(
        local,
        mesh=mesh,
        in_specs=(row, row, row, P("ctx"), pre, pre, weight, weight, weight, col, col, col),
        out_specs=(col, col, col, weight),
        check_vma=False,
    )
```

```python
import jax
import jax.numpy as jnp
from jax import lax
from jax.experimental import pallas as pl
from jax.experimental.pallas import tpu as pltpu
from jax.sharding import PartitionSpec as P

HEAD_DIM = 128
MESH = pl.DeviceIdType.MESH
BF16, F32, I32 = jnp.bfloat16, jnp.float32, jnp.int32
OWNERS, GROUPS = 32, 8
SLOTS, TOKENS, WIDTH, HIDDEN = 48, 256, 2048, 256
TAKE, SHARE = 1280, 768
FIRST, SPAN, BLOCKS = WIDTH - TAKE, 256, TAKE // 256
STEP = 4
STEPS, ROWS = OWNERS // STEP, STEP * SLOTS
REACH = 7


def dot(a, b, dims):
    return lax.dot_general(a, b, (dims, ((), ())), preferred_element_type=F32)


def place(me):
    return me // 8, (me // 2) % 4, me % 2


def offset(slot):
    o = (11 * slot) % 32
    return o // 8, (o // 2) % 4, o % 2


def dest(me, slot):
    (y, x, c), (dy, dx, dc) = place(me), offset(slot)
    a, b = dy + c * (dx - dy), dx + c * (dy - dx)
    return ((y + a) % 4) * 8 + ((x + b) % 4) * 2 + (c + dc) % 2


def source(me, slot):
    (y, x, c), (dy, dx, dc) = place(me), offset(slot)
    s = (c + dc) % 2
    a, b = dy + s * (dx - dy), dx + s * (dy - dx)
    return ((y + 4 - a) % 4) * 8 + ((x + 4 - b) % 4) * 2 + s


def kernel(
    rank, gate, rows_in, gate_pre, up_pre, w_gate, w_up, w_down, q_ref, k_ref, v_ref, seg_row, seg_col, ends,
    q_out, k_out, v_out, down_out,
    send, cot, part, part_in, back, got, hidden, y_sum, y_out, y_in, y_acc, state_out, state_in, ends_in, scores, carried,
    send_s, send_r, pass_s, pass_r, pair_s, pair_r, back_s, back_r, y_s, y_r, state_s, state_r, ends_s, ends_r,
):
    me, z = lax.axis_index("ctx"), lax.axis_index("ep")
    half = z % 2
    mate = z + 1 - 2 * half
    base = pl.multiple_of(half * FIRST, 128)
    mine = pl.multiple_of(half * TAKE, 128)
    theirs = pl.multiple_of((1 - half) * TAKE, 128)

    def remote(src, dst, s, r, ctx, ep):
        return pltpu.make_async_remote_copy(src, dst, s, r, device_id=(ctx, ep), device_id_type=MESH)

    def sending(i):
        return remote(send.at[i], cot.at[i, :, pl.ds(base, TAKE)], send_s.at[i], send_r.at[i], dest(me, i), z)

    def passing(i):
        columns = cot.at[i, :, pl.ds(mine, SHARE)]
        return remote(columns, columns, pass_s.at[i], pass_r.at[i], me, mate)

    def passed(i):
        columns = cot.at[i, :, pl.ds(theirs, SHARE)]
        return remote(columns, columns, pass_s.at[i], pass_r.at[i], me, mate)

    def pairing(i):
        return remote(part.at[i, :, pl.ds(theirs, SHARE)], part_in.at[i], pair_s.at[i], pair_r.at[i], me, mate)

    def returning(i):
        return remote(back.at[i], got.at[i], back_s.at[i], back_r.at[i], source(me, i), z)

    def shard(j):
        return (me + 1 + j) % OWNERS if j < REACH else (me + OWNERS - (j - REACH + 1)) % OWNERS

    def telling(j):
        return remote(ends, ends_in.at[j], ends_s.at[j], ends_r.at[j], shard(j), z)

    def stating(j):
        return remote(state_out.at[j // REACH], state_in.at[j], state_s.at[j], state_r.at[j], shard(j), z)

    barrier = pltpu.get_barrier_semaphore()

    @pl.loop(1, OWNERS)
    def _(i):
        pl.semaphore_signal(barrier, 1, device_id=((me + i) % OWNERS, z), device_id_type=MESH)

    @pl.loop(1, GROUPS)
    def _(i):
        pl.semaphore_signal(barrier, 1, device_id=(me, (z + i) % GROUPS), device_id_type=MESH)

    slot_of = lax.broadcasted_iota(I32, (SLOTS, TOKENS), 0).astype(F32)

    def seats(g, weighted):
        blocks = []
        for j in range(STEP):
            seated = slot_of == rank[g * STEP + j]
            blocks.append(jnp.where(seated, gate[g * STEP + j] if weighted else 1.0, 0.0).astype(BF16))
        return jnp.concatenate(blocks, axis=0)

    def fill(g):
        made = dot(seats(g, True), rows_in[:, pl.ds(base, TAKE)], ((1,), (0,)))
        send[pl.ds(g * STEP, STEP)] = made.astype(BF16).reshape(STEP, SLOTS, TAKE)

    fill(0)
    pl.semaphore_wait(barrier, OWNERS + GROUPS - 2)

    for j in range(2 * REACH):
        telling(j).start()

    @pl.loop(0, STEPS)
    def _(g):
        @pl.when(g > 0)
        def _():
            fill(g)

        for j in range(STEP):

            @pl.when(g * STEP + j > 0)
            def _():
                sending(g * STEP + j).start()

    own = jnp.where(slot_of == rank[0], gate[0], 0.0).astype(BF16)
    cot[0] = dot(own, rows_in[...], ((1,), (0,))).astype(BF16)

    first_mask = seg_col[...] == ends[0:1, :]
    last_mask = seg_col[...] == ends[8:9, :]
    for h in range(2):
        head = slice(h * HEAD_DIM, (h + 1) * HEAD_DIM)
        held = jnp.where(last_mask, k_ref[:, head].astype(F32), 0.0).astype(BF16)
        state_out[0, h] = dot(held, v_ref[:, head], ((0,), (0,))).astype(BF16)
    for j in range(REACH):
        stating(j).start()

    def experts(g):
        these = pl.ds(g * STEP, STEP)
        rows = cot[these].reshape(ROWS, WIDTH)
        down_part = dot(rows, w_down[0], ((1,), (1,)))
        a = jnp.concatenate([gate_pre[0, source(me, g * STEP + j)] for j in range(STEP)], axis=0).astype(F32)
        u = jnp.concatenate([up_pre[0, source(me, g * STEP + j)] for j in range(STEP)], axis=0).astype(F32)
        s = jax.nn.sigmoid(a)
        hidden[pl.ds(g * ROWS, ROWS), :] = (a * s * u).astype(BF16)
        gate_delta = (down_part * u * s * (1.0 + a * (1.0 - s))).astype(BF16)
        up_delta = (down_part * a * s).astype(BF16)
        for n in range(WIDTH // 512):
            columns = slice(n * 512, (n + 1) * 512)
            total = dot(gate_delta, w_gate[0, columns, :], ((1,), (1,)))
            total += dot(up_delta, w_up[0, columns, :], ((1,), (1,)))
            part[these, :, columns] = total.astype(BF16).reshape(STEP, SLOTS, 512)

    @pl.loop(0, STEPS + 2)
    def _(t):
        @pl.when(t < STEPS)
        def _():
            for j in range(STEP):

                @pl.when(t * STEP + j > 0)
                def _():
                    sending(t * STEP + j).wait_recv()
                    passing(t * STEP + j).start()

        @pl.when((t > 0) & (t < STEPS + 1))
        def _():
            g = t - 1
            for j in range(STEP):

                @pl.when(g * STEP + j > 0)
                def _():
                    passed(g * STEP + j).wait_recv()

            experts(g)
            for j in range(STEP):
                pairing(g * STEP + j).start()

        @pl.when(t > 1)
        def _():
            g = t - 2
            for j in range(STEP):
                pairing(g * STEP + j).wait_recv()
            these = pl.ds(g * STEP, STEP)
            shared = pl.multiple_of(half * (TAKE - SHARE), 128)
            both = pl.multiple_of((1 - half) * SHARE, 128)
            summed = part[these, :, pl.ds(mine, SHARE)].astype(F32) + part_in[these].astype(F32)
            back[these, :, pl.ds(shared, SHARE)] = summed.astype(BF16)
            back[these, :, pl.ds(both, TAKE - SHARE)] = part[these, :, pl.ds(SHARE, TAKE - SHARE)]
            for j in range(STEP):

                @pl.when(g * STEP + j > 0)
                def _():
                    returning(g * STEP + j).start()

    got[0] = back[0]
    for n in range(WIDTH // 256):
        columns = slice(n * 256, (n + 1) * 256)
        down_out[0, :, columns] = dot(
            hidden[...], cot[:, :, columns].reshape(OWNERS * SLOTS, 256), ((0,), (0,))
        )

    rows_at = lax.broadcasted_iota(I32, (TOKENS, TOKENS), 0)
    cols_at = lax.broadcasted_iota(I32, (TOKENS, TOKENS), 1)
    allowed = (rows_at >= cols_at) & (jnp.concatenate([seg_col[...]] * 2, axis=1) == seg_row[0:1, :])

    def arrived(backward):
        total = jnp.zeros((2, HEAD_DIM, HEAD_DIM), F32)
        for j in range(REACH):
            k = backward * REACH + j
            stating(k).wait_recv()
            if backward:
                same = ends_in[k, 0:1, :] == ends[8:9, :]
                inside = jnp.where(me + 1 + j < OWNERS, 1.0, 0.0)
            else:
                same = ends_in[k, 8:9, :] == ends[0:1, :]
                inside = jnp.where(me - 1 - j >= 0, 1.0, 0.0)
            weight = jnp.where(same, 1.0, 0.0) * inside
            total += state_in[k].astype(F32) * weight[None]
        return total.astype(BF16)

    for j in range(2 * REACH):
        telling(j).wait_recv()
    carried[...] = arrived(0)
    for h in range(2):
        head = slice(h * HEAD_DIM, (h + 1) * HEAD_DIM)
        scores[h] = jnp.where(allowed, dot(q_ref[:, head], k_ref[:, head], ((1,), (1,))), 0.0).astype(BF16)

    y_sum[...] = jnp.zeros_like(y_sum)

    @pl.loop(0, STEPS)
    def _(g):
        for j in range(STEP):

            @pl.when(g * STEP + j > 0)
            def _():
                returning(g * STEP + j).wait_recv()

        rows = got[pl.ds(g * STEP, STEP)].reshape(ROWS, TAKE)
        y_sum[...] += dot(seats(g, False), rows, ((0,), (0,)))

    def spreading(b):
        to = 3 * half + b
        return remote(y_out.at[b], y_in.at[z], y_s.at[b], y_r.at[z], me, to)

    def spread(i):
        return remote(y_out.at[0], y_in.at[i], y_s.at[0], y_r.at[i], me, z)

    y_acc[...] = jnp.zeros_like(y_acc)
    for b in range(BLOCKS):
        block = y_sum[:, b * SPAN : (b + 1) * SPAN]
        y_out[b] = block.astype(BF16)

        @pl.when(3 * half + b != z)
        def _():
            spreading(b).start()

        @pl.when(3 * half + b == z)
        def _():
            y_acc[...] = y_sum[:, b * SPAN : (b + 1) * SPAN]

    for i in range(GROUPS):
        low = 3 * (i % 2)

        @pl.when((z != i) & (z >= low) & (z < low + BLOCKS))
        def _():
            spread(i).wait_recv()
            y_acc[...] += y_in[i].astype(F32)

    for h in range(2):
        head = slice(h * HEAD_DIM, (h + 1) * HEAD_DIM)
        opened = jnp.where(first_mask, q_ref[:, head].astype(F32), 0.0).astype(BF16)
        state_out[1, h] = dot(opened, y_acc[:, head].astype(BF16), ((0,), (0,))).astype(BF16)
    for j in range(REACH, 2 * REACH):
        stating(j).start()

    inner = []
    for h in range(2):
        head = slice(h * HEAD_DIM, (h + 1) * HEAD_DIM)
        g_h = y_acc[:, head].astype(BF16)
        cot_value = jnp.where(allowed, dot(g_h, v_ref[:, head], ((1,), (1,))), 0.0).astype(BF16)
        query_grad = dot(cot_value, k_ref[:, head], ((1,), (0,)))
        query_grad += jnp.where(first_mask, dot(g_h, carried[h], ((1,), (1,))), 0.0)
        q_out[:, head] = query_grad.astype(BF16)
        inner.append((dot(cot_value, q_ref[:, head], ((0,), (0,))), dot(scores[h], g_h, ((0,), (0,)))))

    back_state = arrived(1)
    for h in range(2):
        head = slice(h * HEAD_DIM, (h + 1) * HEAD_DIM)
        key_grad, value_grad = inner[h]
        key_part = dot(v_ref[:, head], back_state[h], ((1,), (1,)))
        value_part = dot(k_ref[:, head], back_state[h], ((1,), (0,)))
        k_out[:, head] = (key_grad + jnp.where(last_mask, key_part, 0.0)).astype(BF16)
        v_out[:, head] = (value_grad + jnp.where(last_mask, value_part, 0.0)).astype(BF16)

    pairing(0).wait_send()

    @pl.loop(1, OWNERS)
    def _(i):
        sending(i).wait_send()
        passing(i).wait_send()
        pairing(i).wait_send()
        returning(i).wait_send()

    for b in range(BLOCKS):

        @pl.when(3 * half + b != z)
        def _():
            spreading(b).wait_send()

    for j in range(2 * REACH):
        telling(j).wait_send()
        stating(j).wait_send()


def local(
    out_grad, gate_values, expert_ids, segment_ids, gate_pre, up_pre, w_gate, w_up, w_down, queries, keys, values
):
    me = lax.axis_index("ctx")
    parity = lax.axis_index("ep") // (GROUPS // 2)
    experts = 2 * dest(me, jnp.arange(OWNERS, dtype=I32)) + parity
    hit = expert_ids.T[:, None, :] == experts[None, :, None]
    named = jnp.any(hit, axis=0)
    gate = jnp.sum(jnp.where(hit, gate_values.T.astype(F32)[:, None, :], 0.0), axis=0)
    places = jnp.arange(TOKENS, dtype=I32)
    earlier = (places[:, None] < places[None, :]).astype(BF16)
    rank = jnp.where(named, dot(named.astype(BF16), earlier, ((1,), (0,))), -1.0)
    seg_row = jnp.broadcast_to(segment_ids[None, :], (8, TOKENS))
    seg_col = jnp.broadcast_to(segment_ids[:, None], (TOKENS, 128))
    ends = jnp.concatenate([jnp.full((8, 128), segment_ids[0]), jnp.full((8, 128), segment_ids[-1])], axis=0)

    vmem = pl.BlockSpec(memory_space=pltpu.VMEM)
    dma = pltpu.SemaphoreType.DMA
    small = jax.ShapeDtypeStruct((TOKENS, SPAN), BF16)
    states = (2, HEAD_DIM, HEAD_DIM)
    return pl.pallas_call(
        kernel,
        out_shape=(small, small, small, jax.ShapeDtypeStruct((1, HIDDEN, WIDTH), F32)),
        in_specs=[vmem] * 14,
        out_specs=(vmem,) * 4,
        scratch_shapes=[
            pltpu.VMEM((OWNERS, SLOTS, TAKE), BF16),
            pltpu.VMEM((OWNERS, SLOTS, WIDTH), BF16),
            pltpu.VMEM((OWNERS, SLOTS, WIDTH), BF16),
            pltpu.VMEM((OWNERS, SLOTS, SHARE), BF16),
            pltpu.VMEM((OWNERS, SLOTS, TAKE), BF16),
            pltpu.VMEM((OWNERS, SLOTS, TAKE), BF16),
            pltpu.VMEM((OWNERS * SLOTS, HIDDEN), BF16),
            pltpu.VMEM((TOKENS, TAKE), F32),
            pltpu.VMEM((BLOCKS, TOKENS, SPAN), BF16),
            pltpu.VMEM((GROUPS, TOKENS, SPAN), BF16),
            pltpu.VMEM((TOKENS, SPAN), F32),
            pltpu.VMEM((2, *states), BF16),
            pltpu.VMEM((2 * REACH, *states), BF16),
            pltpu.VMEM((2 * REACH, 16, 128), I32),
            pltpu.VMEM((2, TOKENS, TOKENS), BF16),
            pltpu.VMEM(states, BF16),
            *[dma((OWNERS,))] * 8,
            dma((BLOCKS,)), dma((GROUPS,)), *[dma((2 * REACH,))] * 4,
        ],
        compiler_params=pltpu.CompilerParams(
            collective_id=0, has_side_effects=True, vmem_limit_bytes=58 << 20
        ),
    )(
        rank[:, None, :], gate[:, None, :], out_grad, gate_pre, up_pre, w_gate, w_up, w_down,
        queries, keys, values, seg_row, seg_col, ends,
    )


def solution(mesh):
    row, col = P("ctx", None), P("ctx", "ep")
    both = ("ctx", "ep")
    pre, weight = P(both, None, None, None), P(both, None, None)
    return jax.shard_map(
        local,
        mesh=mesh,
        in_specs=(row, row, row, P("ctx"), pre, pre, weight, weight, weight, col, col, col),
        out_specs=(col, col, col, weight),
        check_vma=False,
    )
```

```python
import jax
import jax.numpy as jnp
from jax import lax
from jax.experimental import pallas as pl
from jax.experimental.pallas import tpu as pltpu
from jax.sharding import PartitionSpec as P

HEAD_DIM = 128
MESH = pl.DeviceIdType.MESH
BF16, F32, I32 = jnp.bfloat16, jnp.float32, jnp.int32
OWNERS, GROUPS = 32, 8
SLOTS, TOKENS, WIDTH, HIDDEN = 48, 256, 2048, 256
GIVE, PASS = 1536, 512
TAKE, SHARE = 1280, 768
SPAN = 256
LAID = (0, 4, 6, 2, 7, 1, 3, 5)
DIRECT, OWN = (TAKE - SHARE) // SPAN, SHARE // SPAN
STEP = 2
STEPS, ROWS = OWNERS // STEP, STEP * SLOTS
HOLD = 2
REACH = 7


def dot(a, b, dims):
    return lax.dot_general(a, b, (dims, ((), ())), preferred_element_type=F32)


def place(me):
    return me // 8, (me // 2) % 4, me % 2


def offset(slot):
    o = (13 * slot) % 32
    return o // 8, (o // 2) % 4, o % 2


def owner_vector(me, slots):
    (y, x, c), o = place(me), (13 * slots) & 31
    dy, dx, dc = o >> 3, (o >> 1) & 3, o & 1
    a, b = dy + c * (dx - dy), dx + c * (dy - dx)
    return ((y + a) & 3) * 8 + ((x + b) & 3) * 2 + ((c + dc) & 1)


def dest(me, slot):
    (y, x, c), (dy, dx, dc) = place(me), offset(slot)
    a, b = dy + c * (dx - dy), dx + c * (dy - dx)
    return ((y + a) % 4) * 8 + ((x + b) % 4) * 2 + (c + dc) % 2


def source(me, slot):
    (y, x, c), (dy, dx, dc) = place(me), offset(slot)
    s = (c + dc) % 2
    a, b = dy + s * (dx - dy), dx + s * (dy - dx)
    return ((y + 4 - a) % 4) * 8 + ((x + 4 - b) % 4) * 2 + s


def kernel(
    ids, gates, segment, rows_in, gate_pre, up_pre, w_gate, w_up, w_down, q_ref, k_ref, v_ref,
    small_out, down_out,
    rank, gate, ends, seg_col, send, cot, part, part_in, back, got, got_direct, hidden, y_sum, y_out, y_in, y_acc, state_out, state_in, ends_in, scores, carried,
    send_s, send_r, pass_s, pass_r, pair_s, pair_r, back_s, back_r, direct_s, direct_r, y_s, y_r, state_s, state_r, ends_s, ends_r,
):
    me, z = lax.axis_index("ctx"), lax.axis_index("ep")
    half = z % 2
    mate = z + 1 - 2 * half
    base = pl.multiple_of(half * (WIDTH - GIVE), 128)
    mine = pl.multiple_of(half * TAKE, 128)
    theirs = pl.multiple_of((1 - half) * TAKE, 128)

    def remote(src, dst, s, r, ctx, ep):
        return pltpu.make_async_remote_copy(src, dst, s, r, device_id=(ctx, ep), device_id_type=MESH)

    def sending(i):
        return remote(send.at[i], cot.at[i, :, pl.ds(base, GIVE)], send_s.at[i], send_r.at[i], dest(me, i), z)

    def passing(i):
        columns = cot.at[i, :, pl.ds(pl.multiple_of(half * GIVE, 128), PASS)]
        return remote(columns, columns, pass_s.at[i], pass_r.at[i], me, mate)

    def passed(i):
        columns = cot.at[i, :, pl.ds(pl.multiple_of((1 - half) * GIVE, 128), PASS)]
        return remote(columns, columns, pass_s.at[i], pass_r.at[i], me, mate)

    def pairing(i):
        return remote(part.at[i, :, pl.ds(theirs, SHARE)], part_in.at[i], pair_s.at[i], pair_r.at[i], me, mate)

    def returning(i):
        return remote(back.at[i], got.at[i], back_s.at[i], back_r.at[i], source(me, i), z)

    def directing(i):
        columns = part.at[i, :, pl.ds(SHARE, TAKE - SHARE)]
        return remote(columns, got_direct.at[i], direct_s.at[i], direct_r.at[i], source(me, i), z)

    def shard(j):
        return (me + 1 + j) % OWNERS if j < REACH else (me + OWNERS - (j - REACH + 1)) % OWNERS

    def telling(j):
        return remote(ends, ends_in.at[j], ends_s.at[j], ends_r.at[j], shard(j), z)

    def stating(j):
        return remote(state_out.at[j // REACH], state_in.at[j], state_s.at[j], state_r.at[j], shard(j), z)

    barrier = pltpu.get_barrier_semaphore()

    @pl.loop(1, OWNERS)
    def _(i):
        pl.semaphore_signal(barrier, 1, device_id=((me + i) % OWNERS, z), device_id_type=MESH)

    @pl.loop(1, GROUPS)
    def _(i):
        pl.semaphore_signal(barrier, 1, device_id=(me, (z + i) % GROUPS), device_id_type=MESH)

    rows_at = lax.broadcasted_iota(I32, (TOKENS, TOKENS), 0)
    cols_at = lax.broadcasted_iota(I32, (TOKENS, TOKENS), 1)
    experts_at = 2 * owner_vector(me, lax.broadcasted_iota(I32, (OWNERS, TOKENS), 0)) + z // (GROUPS // 2)
    named = jnp.zeros((OWNERS, TOKENS), F32)
    weight_of = jnp.zeros((OWNERS, TOKENS), F32)
    for k in range(ids.shape[0]):
        hit = ids[k : k + 1, :] == experts_at
        named = jnp.where(hit, 1.0, named)
        weight_of = jnp.where(hit, gates[k : k + 1, :].astype(F32), weight_of)
    before = dot(named.astype(BF16), jnp.where(rows_at < cols_at, 1.0, 0.0).astype(BF16), ((1,), (0,)))
    rank[...] = jnp.where(named > 0.0, before, -1.0)
    gate[...] = weight_of
    seg_row = segment[...].astype(F32)
    seg_col[...] = jnp.transpose(jnp.broadcast_to(seg_row, (128, TOKENS)))
    ends[0:8, :] = jnp.broadcast_to(seg_col[0:1, :], (8, 128))
    ends[8:16, :] = jnp.broadcast_to(seg_col[TOKENS - 1 : TOKENS, :], (8, 128))
    slot_of = lax.broadcasted_iota(I32, (SLOTS, TOKENS), 0).astype(F32)

    def seats(g, weighted):
        blocks = []
        for j in range(STEP):
            at = pl.ds(g * STEP + j, 1)
            seated = slot_of == rank[at, :]
            blocks.append(jnp.where(seated, gate[at, :] if weighted else 1.0, 0.0).astype(BF16))
        return jnp.concatenate(blocks, axis=0)

    def fill(g):
        made = dot(seats(g, True), rows_in[:, pl.ds(base, GIVE)], ((1,), (0,)))
        send[pl.ds(g * STEP, STEP)] = made.astype(BF16).reshape(STEP, SLOTS, GIVE)

    fill(0)
    pl.semaphore_wait(barrier, OWNERS + GROUPS - 2)

    for j in range(2 * REACH):
        telling(j).start()

    @pl.loop(0, STEPS)
    def _(g):
        @pl.when(g > 0)
        def _():
            fill(g)

        for j in range(STEP):

            @pl.when(g * STEP + j > 0)
            def _():
                sending(g * STEP + j).start()

    own = jnp.where(slot_of == rank[0:1, :], gate[0:1, :], 0.0).astype(BF16)
    cot[0] = dot(own, rows_in[...], ((1,), (0,))).astype(BF16)

    first_mask = seg_col[...] == ends[0:1, :]
    last_mask = seg_col[...] == ends[8:9, :]
    for h in range(2):
        head = slice(h * HEAD_DIM, (h + 1) * HEAD_DIM)
        held = jnp.where(last_mask, k_ref[:, head].astype(F32), 0.0).astype(BF16)
        state_out[0, h] = dot(held, v_ref[:, head], ((0,), (0,))).astype(BF16)
    for j in range(REACH):
        stating(j).start()

    def experts(g):
        these = pl.ds(g * STEP, STEP)
        rows = cot[these].reshape(ROWS, WIDTH)
        down_part = dot(rows, w_down[0], ((1,), (1,)))
        a = jnp.concatenate([gate_pre[0, source(me, g * STEP + j)] for j in range(STEP)], axis=0).astype(F32)
        u = jnp.concatenate([up_pre[0, source(me, g * STEP + j)] for j in range(STEP)], axis=0).astype(F32)
        s = jax.nn.sigmoid(a)
        hidden[pl.ds(g * ROWS, ROWS), :] = (a * s * u).astype(BF16)
        gate_delta = (down_part * u * s * (1.0 + a * (1.0 - s))).astype(BF16)
        up_delta = (down_part * a * s).astype(BF16)
        for n in (3, 4, 0, 1, 2, 5, 6, 7):
            columns = slice(LAID[n] * SPAN, (LAID[n] + 1) * SPAN)
            total = dot(gate_delta, w_gate[0, columns, :], ((1,), (1,)))
            total += dot(up_delta, w_up[0, columns, :], ((1,), (1,)))
            part[these, :, n * SPAN : (n + 1) * SPAN] = total.astype(BF16).reshape(STEP, SLOTS, SPAN)

    @pl.loop(0, STEPS + 2)
    def _(t):
        @pl.when(t < STEPS)
        def _():
            for j in range(STEP):

                @pl.when(t * STEP + j > 0)
                def _():
                    sending(t * STEP + j).wait_recv()
                    passing(t * STEP + j).start()

        @pl.when((t > 0) & (t < STEPS + 1))
        def _():
            g = t - 1
            for j in range(STEP):

                @pl.when(g * STEP + j > 0)
                def _():
                    passed(g * STEP + j).wait_recv()

            experts(g)
            for j in range(STEP):
                pairing(g * STEP + j).start()

                @pl.when(g * STEP + j > 0)
                def _():
                    directing(g * STEP + j).start()

        @pl.when(t > 1)
        def _():
            g = t - 2
            for j in range(STEP):
                pairing(g * STEP + j).wait_recv()
            these = pl.ds(g * STEP, STEP)
            summed = part[these, :, pl.ds(mine, SHARE)].astype(F32) + part_in[these].astype(F32)
            back[these] = summed.astype(BF16)

            @pl.when(t >= HOLD)
            def _():
                for j in range(STEP):

                    @pl.when(g * STEP + j > 0)
                    def _():
                        returning(g * STEP + j).start()

        @pl.when(t == HOLD)
        def _():
            @pl.loop(1, (HOLD - 2) * STEP)
            def _(i):
                returning(i).start()

    got[0] = back[0]
    got_direct[0] = part[0, :, SHARE:TAKE]

    allowed = (rows_at >= cols_at) & (jnp.concatenate([seg_col[...]] * 2, axis=1) == seg_row)

    def arrived(backward):
        total = jnp.zeros((2, HEAD_DIM, HEAD_DIM), F32)
        for j in range(REACH):
            k = backward * REACH + j
            stating(k).wait_recv()
            if backward:
                same = ends_in[k, 0:1, :] == ends[8:9, :]
                inside = jnp.where(me + 1 + j < OWNERS, 1.0, 0.0)
            else:
                same = ends_in[k, 8:9, :] == ends[0:1, :]
                inside = jnp.where(me - 1 - j >= 0, 1.0, 0.0)
            weight = jnp.where(same, 1.0, 0.0) * inside
            total += state_in[k].astype(F32) * weight[None]
        return total.astype(BF16)

    for j in range(2 * REACH):
        telling(j).wait_recv()
    carried[...] = arrived(0)
    for h in range(2):
        head = slice(h * HEAD_DIM, (h + 1) * HEAD_DIM)
        scores[h] = jnp.where(allowed, dot(q_ref[:, head], k_ref[:, head], ((1,), (1,))), 0.0).astype(BF16)

    y_acc[...] = jnp.zeros_like(y_acc)

    def spreading(b, to):
        return remote(y_out.at[b], y_in.at[z], y_s.at[b], y_r.at[z], me, to)

    def spread(i):
        return remote(y_out.at[0], y_in.at[i], y_s.at[0], y_r.at[i], me, z)

    def out_of(b, to):
        @pl.when(to != z)
        def _():
            spreading(b, to).start()

        @pl.when(to == z)
        def _():
            y_acc[...] = y_sum[:, b * SPAN : (b + 1) * SPAN]

    y_sum[...] = jnp.zeros_like(y_sum)

    @pl.loop(0, STEPS)
    def _(g):
        for j in range(STEP):

            @pl.when(g * STEP + j > 0)
            def _():
                directing(g * STEP + j).wait_recv()

        rows = got_direct[pl.ds(g * STEP, STEP)].reshape(ROWS, TAKE - SHARE)
        y_sum[:, 0 : TAKE - SHARE] += dot(seats(g, False), rows, ((0,), (0,)))

    for b in range(DIRECT):
        y_out[b] = y_sum[:, b * SPAN : (b + 1) * SPAN].astype(BF16)
        out_of(b, LAID[OWN + b])

    for n in range(WIDTH // 256):
        columns = slice(n * 256, (n + 1) * 256)
        down_out[0, :, columns] = dot(
            hidden[...], cot[:, :, columns].reshape(OWNERS * SLOTS, 256), ((0,), (0,))
        )

    @pl.loop(0, STEPS)
    def _(g):
        for j in range(STEP):

            @pl.when(g * STEP + j > 0)
            def _():
                returning(g * STEP + j).wait_recv()

        rows = got[pl.ds(g * STEP, STEP)].reshape(ROWS, SHARE)
        y_sum[:, TAKE - SHARE : TAKE] += dot(seats(g, False), rows, ((0,), (0,)))

    for b in range(OWN):
        y_out[DIRECT + b] = y_sum[:, (DIRECT + b) * SPAN : (DIRECT + b + 1) * SPAN].astype(BF16)
        even, odd = LAID[b], LAID[OWN + DIRECT + b]
        out_of(DIRECT + b, even + half * (odd - even))

    is_direct = (z == LAID[OWN]) | (z == LAID[OWN + 1])
    odd_own = (z == LAID[5]) | (z == LAID[6]) | (z == LAID[7])
    for i in range(GROUPS):
        wanted = is_direct | odd_own if i % 2 else jnp.logical_not(odd_own)

        @pl.when((z != i) & wanted)
        def _():
            spread(i).wait_recv()
            y_acc[...] += y_in[i].astype(F32)

    for h in range(2):
        head = slice(h * HEAD_DIM, (h + 1) * HEAD_DIM)
        opened = jnp.where(first_mask, q_ref[:, head].astype(F32), 0.0).astype(BF16)
        state_out[1, h] = dot(opened, y_acc[:, head].astype(BF16), ((0,), (0,))).astype(BF16)
    for j in range(REACH, 2 * REACH):
        stating(j).start()

    inner = []
    for h in range(2):
        head = slice(h * HEAD_DIM, (h + 1) * HEAD_DIM)
        g_h = y_acc[:, head].astype(BF16)
        cot_value = jnp.where(allowed, dot(g_h, v_ref[:, head], ((1,), (1,))), 0.0).astype(BF16)
        query_grad = dot(cot_value, k_ref[:, head], ((1,), (0,)))
        query_grad += jnp.where(first_mask, dot(g_h, carried[h], ((1,), (1,))), 0.0)
        small_out[0, :, head] = query_grad.astype(BF16)
        inner.append((dot(cot_value, q_ref[:, head], ((0,), (0,))), dot(scores[h], g_h, ((0,), (0,)))))

    back_state = arrived(1)
    for h in range(2):
        head = slice(h * HEAD_DIM, (h + 1) * HEAD_DIM)
        key_grad, value_grad = inner[h]
        key_part = dot(v_ref[:, head], back_state[h], ((1,), (1,)))
        value_part = dot(k_ref[:, head], back_state[h], ((1,), (0,)))
        small_out[1, :, head] = (key_grad + jnp.where(last_mask, key_part, 0.0)).astype(BF16)
        small_out[2, :, head] = (value_grad + jnp.where(last_mask, value_part, 0.0)).astype(BF16)

    pairing(0).wait_send()

    @pl.loop(1, OWNERS)
    def _(i):
        sending(i).wait_send()
        passing(i).wait_send()
        pairing(i).wait_send()
        returning(i).wait_send()
        directing(i).wait_send()

    for b in range(DIRECT + OWN):
        if b < DIRECT:
            to = LAID[OWN + b]
        else:
            to = LAID[b - DIRECT] + half * (LAID[OWN + b] - LAID[b - DIRECT])

        @pl.when(to != z)
        def _():
            spreading(b, to).wait_send()

    for j in range(2 * REACH):
        telling(j).wait_send()
        stating(j).wait_send()


def hand_over(grads, down_grad, q_out, k_out, v_out, down_out):
    for i, out in enumerate((q_out, k_out, v_out)):
        out[...] = grads[i]
    down_out[...] = down_grad[...]


def local(
    out_grad, gate_values, expert_ids, segment_ids, gate_pre, up_pre, w_gate, w_up, w_down, queries, keys, values
):
    vmem = pl.BlockSpec(memory_space=pltpu.VMEM)
    dma = pltpu.SemaphoreType.DMA
    small = jax.ShapeDtypeStruct((3, TOKENS, SPAN), BF16)
    down = jax.ShapeDtypeStruct((1, HIDDEN, WIDTH), F32)
    states = (2, HEAD_DIM, HEAD_DIM)
    grads, down_grad = pl.pallas_call(
        kernel,
        out_shape=(small, down),
        in_specs=[vmem] * 12,
        out_specs=(vmem,) * 2,
        scratch_shapes=[
            pltpu.VMEM((OWNERS, TOKENS), F32),
            pltpu.VMEM((OWNERS, TOKENS), F32),
            pltpu.VMEM((16, 128), F32),
            pltpu.VMEM((TOKENS, 128), F32),
            pltpu.VMEM((OWNERS, SLOTS, GIVE), BF16),
            pltpu.VMEM((OWNERS, SLOTS, WIDTH), BF16),
            pltpu.VMEM((OWNERS, SLOTS, WIDTH), BF16),
            pltpu.VMEM((OWNERS, SLOTS, SHARE), BF16),
            pltpu.VMEM((OWNERS, SLOTS, SHARE), BF16),
            pltpu.VMEM((OWNERS, SLOTS, SHARE), BF16),
            pltpu.VMEM((OWNERS, SLOTS, TAKE - SHARE), BF16),
            pltpu.VMEM((OWNERS * SLOTS, HIDDEN), BF16),
            pltpu.VMEM((TOKENS, TAKE), F32),
            pltpu.VMEM((DIRECT + OWN, TOKENS, SPAN), BF16),
            pltpu.VMEM((GROUPS, TOKENS, SPAN), BF16),
            pltpu.VMEM((TOKENS, SPAN), F32),
            pltpu.VMEM((2, *states), BF16),
            pltpu.VMEM((2 * REACH, *states), BF16),
            pltpu.VMEM((2 * REACH, 16, 128), F32),
            pltpu.VMEM((2, TOKENS, TOKENS), BF16),
            pltpu.VMEM(states, BF16),
            *[dma((OWNERS,))] * 10,
            dma((DIRECT + OWN,)), dma((GROUPS,)), *[dma((2 * REACH,))] * 4,
        ],
        compiler_params=pltpu.CompilerParams(
            collective_id=0, has_side_effects=True, vmem_limit_bytes=58 << 20
        ),
    )(
        expert_ids.T, gate_values.T, segment_ids[None, :], out_grad, gate_pre, up_pre, w_gate, w_up, w_down,
        queries, keys, values,
    )
    one = jax.ShapeDtypeStruct((TOKENS, SPAN), BF16)
    return pl.pallas_call(
        hand_over,
        out_shape=(one, one, one, down),
        in_specs=[vmem, vmem],
        out_specs=(vmem,) * 4,
        compiler_params=pltpu.CompilerParams(vmem_limit_bytes=8 << 20),
    )(grads, down_grad)


def solution(mesh):
    row, col = P("ctx", None), P("ctx", "ep")
    both = ("ctx", "ep")
    pre, weight = P(both, None, None, None), P(both, None, None)
    return jax.shard_map(
        local,
        mesh=mesh,
        in_specs=(row, row, row, P("ctx"), pre, pre, weight, weight, weight, col, col, col),
        out_specs=(col, col, col, weight),
        check_vma=False,
    )
```

```python
import jax
import jax.numpy as jnp
from jax import lax
from jax.experimental import pallas as pl
from jax.experimental.pallas import tpu as pltpu
from jax.sharding import PartitionSpec as P

HEAD_DIM = 128
MESH = pl.DeviceIdType.MESH
BF16, F32, I32 = jnp.bfloat16, jnp.float32, jnp.int32
OWNERS, GROUPS = 32, 8
SLOTS, TOKENS, WIDTH, HIDDEN = 48, 256, 2048, 256
GIVE, PASS = 1536, 512
TAKE, SHARE = 1280, 768
SPAN, PIECE = 256, 64
LAID = (0, 4, 6, 2, 7, 1, 3, 5)
DIRECT, OWN = (TAKE - SHARE) // SPAN, SHARE // SPAN
STEP = 2
STEPS, ROWS = OWNERS // STEP, STEP * SLOTS
LATER, LAST = 2, 4
REACH = 7


def dot(a, b, dims):
    return lax.dot_general(a, b, (dims, ((), ())), preferred_element_type=F32)


def place(me):
    return me // 8, (me // 2) % 4, me % 2


def offset(slot):
    o = (13 * slot) % 32
    return o // 8, (o // 2) % 4, o % 2


def owner_vector(me, slots):
    (y, x, c), o = place(me), (13 * slots) & 31
    dy, dx, dc = o >> 3, (o >> 1) & 3, o & 1
    a, b = dy + c * (dx - dy), dx + c * (dy - dx)
    return ((y + a) & 3) * 8 + ((x + b) & 3) * 2 + ((c + dc) & 1)


def dest(me, slot):
    (y, x, c), (dy, dx, dc) = place(me), offset(slot)
    a, b = dy + c * (dx - dy), dx + c * (dy - dx)
    return ((y + a) % 4) * 8 + ((x + b) % 4) * 2 + (c + dc) % 2


def source(me, slot):
    (y, x, c), (dy, dx, dc) = place(me), offset(slot)
    s = (c + dc) % 2
    a, b = dy + s * (dx - dy), dx + s * (dy - dx)
    return ((y + 4 - a) % 4) * 8 + ((x + 4 - b) % 4) * 2 + s


def kernel(
    ids, gates, segment, rows_in, gate_pre, up_pre, w_gate, w_up, w_down, q_ref, k_ref, v_ref,
    small_out, down_out,
    down, down_s, rank, gate, ends, seg_col, send, cot, part, part_in, back, got, got_direct, hidden, y_sum, y_out, y_in, y_acc, state_out, state_in, ends_in, scores, carried,
    send_s, send_r, pass_s, pass_r, pair_s, pair_r, back_s, back_r, direct_s, direct_r, y_s, y_r, state_s, state_r, ends_s, ends_r,
):
    me, z = lax.axis_index("ctx"), lax.axis_index("ep")
    half = z % 2
    mate = z + 1 - 2 * half
    base = pl.multiple_of(half * (WIDTH - GIVE), 128)
    mine = pl.multiple_of(half * TAKE, 128)
    theirs = pl.multiple_of((1 - half) * TAKE, 128)

    def remote(src, dst, s, r, ctx, ep):
        return pltpu.make_async_remote_copy(src, dst, s, r, device_id=(ctx, ep), device_id_type=MESH)

    def sending(i):
        return remote(send.at[i], cot.at[i, :, pl.ds(base, GIVE)], send_s.at[i], send_r.at[i], dest(me, i), z)

    def passing(i):
        columns = cot.at[i, :, pl.ds(pl.multiple_of(half * GIVE, 128), PASS)]
        return remote(columns, columns, pass_s.at[i], pass_r.at[i], me, mate)

    def passed(i):
        columns = cot.at[i, :, pl.ds(pl.multiple_of((1 - half) * GIVE, 128), PASS)]
        return remote(columns, columns, pass_s.at[i], pass_r.at[i], me, mate)

    def pairing(i):
        return remote(part.at[i, :, pl.ds(theirs, SHARE)], part_in.at[i], pair_s.at[i], pair_r.at[i], me, mate)

    def returning(i):
        return remote(back.at[i], got.at[i], back_s.at[i], back_r.at[i], source(me, i), z)

    def directing(i):
        columns = part.at[i, :, pl.ds(SHARE, TAKE - SHARE)]
        return remote(columns, got_direct.at[i], direct_s.at[i], direct_r.at[i], source(me, i), z)

    def shard(j):
        return (me + 1 + j) % OWNERS if j < REACH else (me + OWNERS - (j - REACH + 1)) % OWNERS

    def telling(j):
        return remote(ends, ends_in.at[j], ends_s.at[j], ends_r.at[j], shard(j), z)

    def stating(j):
        return remote(state_out.at[j // REACH], state_in.at[j], state_s.at[j], state_r.at[j], shard(j), z)

    barrier = pltpu.get_barrier_semaphore()

    @pl.loop(1, OWNERS)
    def _(i):
        pl.semaphore_signal(barrier, 1, device_id=((me + i) % OWNERS, z), device_id_type=MESH)

    @pl.loop(1, GROUPS)
    def _(i):
        pl.semaphore_signal(barrier, 1, device_id=(me, (z + i) % GROUPS), device_id_type=MESH)

    rows_at = lax.broadcasted_iota(I32, (TOKENS, TOKENS), 0)
    cols_at = lax.broadcasted_iota(I32, (TOKENS, TOKENS), 1)
    experts_at = 2 * owner_vector(me, lax.broadcasted_iota(I32, (OWNERS, TOKENS), 0)) + z // (GROUPS // 2)
    named = jnp.zeros((OWNERS, TOKENS), F32)
    weight_of = jnp.zeros((OWNERS, TOKENS), F32)
    for k in range(ids.shape[0]):
        hit = ids[k : k + 1, :] == experts_at
        named = jnp.where(hit, 1.0, named)
        weight_of = jnp.where(hit, gates[k : k + 1, :].astype(F32), weight_of)
    before = dot(named.astype(BF16), jnp.where(rows_at < cols_at, 1.0, 0.0).astype(BF16), ((1,), (0,)))
    rank[...] = jnp.where(named > 0.0, before, -1.0)
    gate[...] = weight_of
    seg_row = segment[...].astype(F32)
    seg_col[...] = jnp.transpose(jnp.broadcast_to(seg_row, (128, TOKENS)))
    ends[0:8, :] = jnp.broadcast_to(seg_col[0:1, :], (8, 128))
    ends[8:16, :] = jnp.broadcast_to(seg_col[TOKENS - 1 : TOKENS, :], (8, 128))
    slot_of = lax.broadcasted_iota(I32, (SLOTS, TOKENS), 0).astype(F32)

    def seats(g, weighted):
        blocks = []
        for j in range(STEP):
            at = pl.ds(g * STEP + j, 1)
            seated = slot_of == rank[at, :]
            blocks.append(jnp.where(seated, gate[at, :] if weighted else 1.0, 0.0).astype(BF16))
        return jnp.concatenate(blocks, axis=0)

    def fill(g):
        made = dot(seats(g, True), rows_in[:, pl.ds(base, GIVE)], ((1,), (0,)))
        send[pl.ds(g * STEP, STEP)] = made.astype(BF16).reshape(STEP, SLOTS, GIVE)

    fill(0)
    pl.semaphore_wait(barrier, OWNERS + GROUPS - 2)

    for j in range(2 * REACH):
        telling(j).start()

    @pl.loop(0, STEPS)
    def _(g):
        @pl.when(g > 0)
        def _():
            fill(g)

        for j in range(STEP):

            @pl.when(g * STEP + j > 0)
            def _():
                sending(g * STEP + j).start()

    own = jnp.where(slot_of == rank[0:1, :], gate[0:1, :], 0.0).astype(BF16)
    cot[0] = dot(own, rows_in[...], ((1,), (0,))).astype(BF16)

    first_mask = seg_col[...] == ends[0:1, :]
    last_mask = seg_col[...] == ends[8:9, :]
    for h in range(2):
        head = slice(h * HEAD_DIM, (h + 1) * HEAD_DIM)
        held = jnp.where(last_mask, k_ref[:, head].astype(F32), 0.0).astype(BF16)
        state_out[0, h] = dot(held, v_ref[:, head], ((0,), (0,))).astype(BF16)
    for j in range(REACH):
        stating(j).start()

    def experts(g):
        these = pl.ds(g * STEP, STEP)
        rows = cot[these].reshape(ROWS, WIDTH)
        down_part = dot(rows, w_down[0], ((1,), (1,)))
        a = jnp.concatenate([gate_pre[0, source(me, g * STEP + j)] for j in range(STEP)], axis=0).astype(F32)
        u = jnp.concatenate([up_pre[0, source(me, g * STEP + j)] for j in range(STEP)], axis=0).astype(F32)
        s = jax.nn.sigmoid(a)
        hidden[pl.ds(g * ROWS, ROWS), :] = (a * s * u).astype(BF16)
        gate_delta = (down_part * u * s * (1.0 + a * (1.0 - s))).astype(BF16)
        up_delta = (down_part * a * s).astype(BF16)
        for n in (3, 4, 0, 1, 2, 5, 6, 7):
            columns = slice(LAID[n] * SPAN, (LAID[n] + 1) * SPAN)
            total = dot(gate_delta, w_gate[0, columns, :], ((1,), (1,)))
            total += dot(up_delta, w_up[0, columns, :], ((1,), (1,)))
            part[these, :, n * SPAN : (n + 1) * SPAN] = total.astype(BF16).reshape(STEP, SLOTS, SPAN)

    @pl.loop(0, STEPS + LAST)
    def _(t):
        @pl.when(t < STEPS)
        def _():
            for j in range(STEP):

                @pl.when(t * STEP + j > 0)
                def _():
                    sending(t * STEP + j).wait_recv()
                    passing(t * STEP + j).start()

        @pl.when((t >= LATER) & (t < STEPS + LATER))
        def _():
            g = t - LATER
            for j in range(STEP):

                @pl.when(g * STEP + j > 0)
                def _():
                    passed(g * STEP + j).wait_recv()

            experts(g)
            for j in range(STEP):
                pairing(g * STEP + j).start()

                @pl.when(g * STEP + j > 0)
                def _():
                    directing(g * STEP + j).start()

        @pl.when(t >= LAST)
        def _():
            g = t - LAST
            for j in range(STEP):
                pairing(g * STEP + j).wait_recv()
            these = pl.ds(g * STEP, STEP)
            summed = part[these, :, pl.ds(mine, SHARE)].astype(F32) + part_in[these].astype(F32)
            back[these] = summed.astype(BF16)

            for j in range(STEP):

                @pl.when(g * STEP + j > 0)
                def _():
                    returning(g * STEP + j).start()

    got[0] = back[0]
    got_direct[0] = part[0, :, SHARE:TAKE]

    allowed = (rows_at >= cols_at) & (jnp.concatenate([seg_col[...]] * 2, axis=1) == seg_row)

    def arrived(backward):
        total = jnp.zeros((2, HEAD_DIM, HEAD_DIM), F32)
        for j in range(REACH):
            k = backward * REACH + j
            stating(k).wait_recv()
            if backward:
                same = ends_in[k, 0:1, :] == ends[8:9, :]
                inside = jnp.where(me + 1 + j < OWNERS, 1.0, 0.0)
            else:
                same = ends_in[k, 8:9, :] == ends[0:1, :]
                inside = jnp.where(me - 1 - j >= 0, 1.0, 0.0)
            weight = jnp.where(same, 1.0, 0.0) * inside
            total += state_in[k].astype(F32) * weight[None]
        return total.astype(BF16)

    for j in range(2 * REACH):
        telling(j).wait_recv()
    carried[...] = arrived(0)
    for h in range(2):
        head = slice(h * HEAD_DIM, (h + 1) * HEAD_DIM)
        scores[h] = jnp.where(allowed, dot(q_ref[:, head], k_ref[:, head], ((1,), (1,))), 0.0).astype(BF16)

    y_acc[...] = jnp.zeros_like(y_acc)

    def spreading(b, to):
        return remote(y_out.at[b], y_in.at[z], y_s.at[b], y_r.at[z], me, to)

    def spread(i):
        return remote(y_out.at[0], y_in.at[i], y_s.at[0], y_r.at[i], me, z)

    def out_of(b, to):
        @pl.when(to != z)
        def _():
            spreading(b, to).start()

        @pl.when(to == z)
        def _():
            y_acc[...] = y_sum[:, b * SPAN : (b + 1) * SPAN]

    y_sum[...] = jnp.zeros_like(y_sum)

    @pl.loop(0, STEPS)
    def _(g):
        for j in range(STEP):

            @pl.when(g * STEP + j > 0)
            def _():
                directing(g * STEP + j).wait_recv()

        rows = got_direct[pl.ds(g * STEP, STEP)].reshape(ROWS, TAKE - SHARE)
        y_sum[:, 0 : TAKE - SHARE] += dot(seats(g, False), rows, ((0,), (0,)))

    for b in range(DIRECT):
        y_out[b] = y_sum[:, b * SPAN : (b + 1) * SPAN].astype(BF16)
        out_of(b, LAID[OWN + b])

    for n in range(WIDTH // 256):
        columns = slice(n * 256, (n + 1) * 256)
        down[:, columns] = dot(
            hidden[...], cot[:, :, columns].reshape(OWNERS * SLOTS, 256), ((0,), (0,))
        )
    writing = pltpu.make_async_copy(down, down_out.at[0], down_s)
    writing.start()

    @pl.loop(0, STEPS)
    def _(g):
        for j in range(STEP):

            @pl.when(g * STEP + j > 0)
            def _():
                returning(g * STEP + j).wait_recv()

        rows = got[pl.ds(g * STEP, STEP)].reshape(ROWS, SHARE)
        y_sum[:, TAKE - SHARE : TAKE] += dot(seats(g, False), rows, ((0,), (0,)))

    for b in range(OWN):
        y_out[DIRECT + b] = y_sum[:, (DIRECT + b) * SPAN : (DIRECT + b + 1) * SPAN].astype(BF16)
        even, odd = LAID[b], LAID[OWN + DIRECT + b]
        out_of(DIRECT + b, even + half * (odd - even))

    is_direct = (z == LAID[OWN]) | (z == LAID[OWN + 1])
    odd_own = (z == LAID[5]) | (z == LAID[6]) | (z == LAID[7])
    for i in range(GROUPS):
        wanted = is_direct | odd_own if i % 2 else jnp.logical_not(odd_own)

        @pl.when((z != i) & wanted)
        def _():
            spread(i).wait_recv()
            y_acc[...] += y_in[i].astype(F32)

    for h in range(2):
        head = slice(h * HEAD_DIM, (h + 1) * HEAD_DIM)
        opened = jnp.where(first_mask, q_ref[:, head].astype(F32), 0.0).astype(BF16)
        state_out[1, h] = dot(opened, y_acc[:, head].astype(BF16), ((0,), (0,))).astype(BF16)
    for j in range(REACH, 2 * REACH):
        stating(j).start()

    inner = []
    for h in range(2):
        head = slice(h * HEAD_DIM, (h + 1) * HEAD_DIM)
        g_h = y_acc[:, head].astype(BF16)
        cot_value = jnp.where(allowed, dot(g_h, v_ref[:, head], ((1,), (1,))), 0.0).astype(BF16)
        query_grad = dot(cot_value, k_ref[:, head], ((1,), (0,)))
        query_grad += jnp.where(first_mask, dot(g_h, carried[h], ((1,), (1,))), 0.0)
        small_out[0, :, head] = query_grad.astype(BF16)
        inner.append((dot(cot_value, q_ref[:, head], ((0,), (0,))), dot(scores[h], g_h, ((0,), (0,)))))

    back_state = arrived(1)
    for h in range(2):
        head = slice(h * HEAD_DIM, (h + 1) * HEAD_DIM)
        key_grad, value_grad = inner[h]
        key_part = dot(v_ref[:, head], back_state[h], ((1,), (1,)))
        value_part = dot(k_ref[:, head], back_state[h], ((1,), (0,)))
        small_out[1, :, head] = (key_grad + jnp.where(last_mask, key_part, 0.0)).astype(BF16)
        small_out[2, :, head] = (value_grad + jnp.where(last_mask, value_part, 0.0)).astype(BF16)

    writing.wait()
    pairing(0).wait_send()

    @pl.loop(1, OWNERS)
    def _(i):
        sending(i).wait_send()
        passing(i).wait_send()
        pairing(i).wait_send()
        returning(i).wait_send()
        directing(i).wait_send()

    for b in range(DIRECT + OWN):
        if b < DIRECT:
            to = LAID[OWN + b]
        else:
            to = LAID[b - DIRECT] + half * (LAID[OWN + b] - LAID[b - DIRECT])

        @pl.when(to != z)
        def _():
            spreading(b, to).wait_send()

    for j in range(2 * REACH):
        telling(j).wait_send()
        stating(j).wait_send()


def hand_over(grads, down_grad, q_out, k_out, v_out, down_out, small, large, come, go):
    count = HIDDEN // PIECE
    pieces = [pl.ds(i * PIECE, PIECE) for i in range(count)]
    chain = [(down_grad.at[0, p], large.at[p], down_out.at[0, p]) for p in pieces]
    chain += [(grads.at[i], small.at[i], out) for i, out in enumerate((q_out, k_out, v_out))]
    into = [pltpu.make_async_copy(a, b, come.at[i]) for i, (a, b, _) in enumerate(chain)]
    out_of = [pltpu.make_async_copy(b, c, go.at[i]) for i, (_, b, c) in enumerate(chain)]
    for copy in into:
        copy.start()
    for first, then in zip(into, out_of):
        first.wait()
        then.start()
    for copy in out_of:
        copy.wait()


def local(
    out_grad, gate_values, expert_ids, segment_ids, gate_pre, up_pre, w_gate, w_up, w_down, queries, keys, values
):
    vmem, hbm = pl.BlockSpec(memory_space=pltpu.VMEM), pl.BlockSpec(memory_space=pl.ANY)
    dma = pltpu.SemaphoreType.DMA
    small = jax.ShapeDtypeStruct((3, TOKENS, SPAN), BF16)
    down = jax.ShapeDtypeStruct((1, HIDDEN, WIDTH), F32)
    states = (2, HEAD_DIM, HEAD_DIM)
    grads, down_grad = pl.pallas_call(
        kernel,
        out_shape=(small, down),
        in_specs=[vmem] * 12,
        out_specs=(vmem, hbm),
        scratch_shapes=[
            pltpu.VMEM((HIDDEN, WIDTH), F32),
            dma,
            pltpu.VMEM((OWNERS, TOKENS), F32),
            pltpu.VMEM((OWNERS, TOKENS), F32),
            pltpu.VMEM((16, 128), F32),
            pltpu.VMEM((TOKENS, 128), F32),
            pltpu.VMEM((OWNERS, SLOTS, GIVE), BF16),
            pltpu.VMEM((OWNERS, SLOTS, WIDTH), BF16),
            pltpu.VMEM((OWNERS, SLOTS, WIDTH), BF16),
            pltpu.VMEM((OWNERS, SLOTS, SHARE), BF16),
            pltpu.VMEM((OWNERS, SLOTS, SHARE), BF16),
            pltpu.VMEM((OWNERS, SLOTS, SHARE), BF16),
            pltpu.VMEM((OWNERS, SLOTS, TAKE - SHARE), BF16),
            pltpu.VMEM((OWNERS * SLOTS, HIDDEN), BF16),
            pltpu.VMEM((TOKENS, TAKE), F32),
            pltpu.VMEM((DIRECT + OWN, TOKENS, SPAN), BF16),
            pltpu.VMEM((GROUPS, TOKENS, SPAN), BF16),
            pltpu.VMEM((TOKENS, SPAN), F32),
            pltpu.VMEM((2, *states), BF16),
            pltpu.VMEM((2 * REACH, *states), BF16),
            pltpu.VMEM((2 * REACH, 16, 128), F32),
            pltpu.VMEM((2, TOKENS, TOKENS), BF16),
            pltpu.VMEM(states, BF16),
            *[dma((OWNERS,))] * 10,
            dma((DIRECT + OWN,)), dma((GROUPS,)), *[dma((2 * REACH,))] * 4,
        ],
        compiler_params=pltpu.CompilerParams(
            collective_id=0, has_side_effects=True, vmem_limit_bytes=58 << 20
        ),
    )(
        expert_ids.T, gate_values.T, segment_ids[None, :], out_grad, gate_pre, up_pre, w_gate, w_up, w_down,
        queries, keys, values,
    )
    one = jax.ShapeDtypeStruct((TOKENS, SPAN), BF16)
    return pl.pallas_call(
        hand_over,
        out_shape=(one, one, one, down),
        in_specs=[hbm, hbm],
        out_specs=(hbm,) * 4,
        scratch_shapes=[
            pltpu.VMEM((3, TOKENS, SPAN), BF16),
            pltpu.VMEM((HIDDEN, WIDTH), F32),
            dma((HIDDEN // PIECE + 3,)),
            dma((HIDDEN // PIECE + 3,)),
        ],
        compiler_params=pltpu.CompilerParams(vmem_limit_bytes=60 << 20),
    )(grads, down_grad)


def solution(mesh):
    row, col = P("ctx", None), P("ctx", "ep")
    both = ("ctx", "ep")
    pre, weight = P(both, None, None, None), P(both, None, None)
    return jax.shard_map(
        local,
        mesh=mesh,
        in_specs=(row, row, row, P("ctx"), pre, pre, weight, weight, weight, col, col, col),
        out_specs=(col, col, col, weight),
        check_vma=False,
    )
```

```python
import jax
import jax.numpy as jnp
from jax import lax
from jax.experimental import pallas as pl
from jax.experimental.pallas import tpu as pltpu
from jax.sharding import PartitionSpec as P

HEAD_DIM = 128
MESH = pl.DeviceIdType.MESH
BF16, F32, I32 = jnp.bfloat16, jnp.float32, jnp.int32
OWNERS, GROUPS = 32, 8
SLOTS, TOKENS, WIDTH, HIDDEN = 48, 256, 2048, 256
GIVE, PASS = 1536, 512
TAKE, SHARE = 1280, 768
SPAN, PIECE = 256, 64
LAID = (0, 4, 6, 2, 7, 1, 3, 5)
DIRECT, OWN = (TAKE - SHARE) // SPAN, SHARE // SPAN
STEP = 2
STEPS, ROWS = OWNERS // STEP, STEP * SLOTS
LATER, LAST = 2, 4
REACH = 7


def dot(a, b, dims):
    return lax.dot_general(a, b, (dims, ((), ())), preferred_element_type=F32)


def place(me):
    return me // 8, (me // 2) % 4, me % 2


def offset(slot):
    o = (13 * slot) % 32
    return o // 8, (o // 2) % 4, o % 2


def owner_vector(me, slots):
    (y, x, c), o = place(me), (13 * slots) & 31
    dy, dx, dc = o >> 3, (o >> 1) & 3, o & 1
    a, b = dy + c * (dx - dy), dx + c * (dy - dx)
    return ((y + a) & 3) * 8 + ((x + b) & 3) * 2 + ((c + dc) & 1)


def dest(me, slot):
    (y, x, c), (dy, dx, dc) = place(me), offset(slot)
    a, b = dy + c * (dx - dy), dx + c * (dy - dx)
    return ((y + a) % 4) * 8 + ((x + b) % 4) * 2 + (c + dc) % 2


def source(me, slot):
    (y, x, c), (dy, dx, dc) = place(me), offset(slot)
    s = (c + dc) % 2
    a, b = dy + s * (dx - dy), dx + s * (dy - dx)
    return ((y + 4 - a) % 4) * 8 + ((x + 4 - b) % 4) * 2 + s


def kernel(
    ids, gates, segment, rows_in, gate_pre, up_pre, w_gate, w_up, w_down, q_ref, k_ref, v_ref,
    small_out, down_out,
    down, down_s, rank, gate, ends, seg_col, send, cot, part, part_in, back, got, got_direct, hidden, y_sum, y_out, y_in, y_acc, state_out, state_in, ends_in, scores, carried,
    send_s, send_r, pass_s, pass_r, pair_s, pair_r, back_s, back_r, direct_s, direct_r, y_s, y_r, state_s, state_r, ends_s, ends_r,
):
    me, z = lax.axis_index("ctx"), lax.axis_index("ep")
    half = z % 2
    mate = z + 1 - 2 * half
    base = pl.multiple_of(half * (WIDTH - GIVE), 128)
    mine = pl.multiple_of(half * TAKE, 128)
    theirs = pl.multiple_of((1 - half) * TAKE, 128)

    def remote(src, dst, s, r, ctx, ep):
        return pltpu.make_async_remote_copy(src, dst, s, r, device_id=(ctx, ep), device_id_type=MESH)

    def sending(i):
        return remote(send.at[i], cot.at[i, :, pl.ds(base, GIVE)], send_s.at[i], send_r.at[i], dest(me, i), z)

    def passing(i):
        columns = cot.at[i, :, pl.ds(pl.multiple_of(half * GIVE, 128), PASS)]
        return remote(columns, columns, pass_s.at[i], pass_r.at[i], me, mate)

    def passed(i):
        columns = cot.at[i, :, pl.ds(pl.multiple_of((1 - half) * GIVE, 128), PASS)]
        return remote(columns, columns, pass_s.at[i], pass_r.at[i], me, mate)

    def pairing(g):
        these = pl.ds(g * STEP, STEP)
        columns = part.at[these, :, pl.ds(theirs, SHARE)]
        return remote(columns, part_in.at[these], pair_s.at[g], pair_r.at[g], me, mate)

    def returning(i):
        return remote(back.at[i], got.at[i], back_s.at[i], back_r.at[i], source(me, i), z)

    def directing(i):
        columns = part.at[i, :, pl.ds(SHARE, TAKE - SHARE)]
        return remote(columns, got_direct.at[i], direct_s.at[i], direct_r.at[i], source(me, i), z)

    def shard(j):
        return (me + 1 + j) % OWNERS if j < REACH else (me + OWNERS - (j - REACH + 1)) % OWNERS

    def telling(j):
        return remote(ends, ends_in.at[j], ends_s.at[j], ends_r.at[j], shard(j), z)

    def stating(j):
        return remote(state_out.at[j // REACH], state_in.at[j], state_s.at[j], state_r.at[j], shard(j), z)

    barrier = pltpu.get_barrier_semaphore()

    @pl.loop(1, OWNERS)
    def _(i):
        pl.semaphore_signal(barrier, 1, device_id=((me + i) % OWNERS, z), device_id_type=MESH)

    @pl.loop(1, GROUPS)
    def _(i):
        pl.semaphore_signal(barrier, 1, device_id=(me, (z + i) % GROUPS), device_id_type=MESH)

    rows_at = lax.broadcasted_iota(I32, (TOKENS, TOKENS), 0)
    cols_at = lax.broadcasted_iota(I32, (TOKENS, TOKENS), 1)
    experts_at = 2 * owner_vector(me, lax.broadcasted_iota(I32, (OWNERS, TOKENS), 0)) + z // (GROUPS // 2)
    named = jnp.zeros((OWNERS, TOKENS), F32)
    weight_of = jnp.zeros((OWNERS, TOKENS), F32)
    for k in range(ids.shape[0]):
        hit = ids[k : k + 1, :] == experts_at
        named = jnp.where(hit, 1.0, named)
        weight_of = jnp.where(hit, gates[k : k + 1, :].astype(F32), weight_of)
    before = dot(named.astype(BF16), jnp.where(rows_at < cols_at, 1.0, 0.0).astype(BF16), ((1,), (0,)))
    rank[...] = jnp.where(named > 0.0, before, -1.0)
    gate[...] = weight_of
    seg_row = segment[...].astype(F32)
    seg_col[...] = jnp.transpose(jnp.broadcast_to(seg_row, (128, TOKENS)))
    ends[0:8, :] = jnp.broadcast_to(seg_col[0:1, :], (8, 128))
    ends[8:16, :] = jnp.broadcast_to(seg_col[TOKENS - 1 : TOKENS, :], (8, 128))
    slot_of = lax.broadcasted_iota(I32, (SLOTS, TOKENS), 0).astype(F32)

    def seats(g, weighted):
        blocks = []
        for j in range(STEP):
            at = pl.ds(g * STEP + j, 1)
            seated = slot_of == rank[at, :]
            blocks.append(jnp.where(seated, gate[at, :] if weighted else 1.0, 0.0).astype(BF16))
        return jnp.concatenate(blocks, axis=0)

    def fill(g):
        made = dot(seats(g, True), rows_in[:, pl.ds(base, GIVE)], ((1,), (0,)))
        send[pl.ds(g * STEP, STEP)] = made.astype(BF16).reshape(STEP, SLOTS, GIVE)

    fill(0)
    pl.semaphore_wait(barrier, OWNERS + GROUPS - 2)

    for j in range(2 * REACH):
        telling(j).start()

    @pl.loop(0, STEPS)
    def _(g):
        @pl.when(g > 0)
        def _():
            fill(g)

        for j in range(STEP):

            @pl.when(g * STEP + j > 0)
            def _():
                sending(g * STEP + j).start()

    own = jnp.where(slot_of == rank[0:1, :], gate[0:1, :], 0.0).astype(BF16)
    cot[0] = dot(own, rows_in[...], ((1,), (0,))).astype(BF16)

    first_mask = seg_col[...] == ends[0:1, :]
    last_mask = seg_col[...] == ends[8:9, :]
    for h in range(2):
        head = slice(h * HEAD_DIM, (h + 1) * HEAD_DIM)
        held = jnp.where(last_mask, k_ref[:, head].astype(F32), 0.0).astype(BF16)
        state_out[0, h] = dot(held, v_ref[:, head], ((0,), (0,))).astype(BF16)
    for j in range(REACH):
        stating(j).start()

    def experts(g):
        these = pl.ds(g * STEP, STEP)
        rows = cot[these].reshape(ROWS, WIDTH)
        down_part = dot(rows, w_down[0], ((1,), (1,)))
        a = jnp.concatenate([gate_pre[0, source(me, g * STEP + j)] for j in range(STEP)], axis=0).astype(F32)
        u = jnp.concatenate([up_pre[0, source(me, g * STEP + j)] for j in range(STEP)], axis=0).astype(F32)
        s = jax.nn.sigmoid(a)
        hidden[pl.ds(g * ROWS, ROWS), :] = (a * s * u).astype(BF16)
        gate_delta = (down_part * u * s * (1.0 + a * (1.0 - s))).astype(BF16)
        up_delta = (down_part * a * s).astype(BF16)
        for n in (3, 4, 0, 1, 2, 5, 6, 7):
            columns = slice(LAID[n] * SPAN, (LAID[n] + 1) * SPAN)
            total = dot(gate_delta, w_gate[0, columns, :], ((1,), (1,)))
            total += dot(up_delta, w_up[0, columns, :], ((1,), (1,)))
            part[these, :, n * SPAN : (n + 1) * SPAN] = total.astype(BF16).reshape(STEP, SLOTS, SPAN)

    @pl.loop(0, STEPS + LAST)
    def _(t):
        @pl.when(t < STEPS)
        def _():
            for j in range(STEP):

                @pl.when(t * STEP + j > 0)
                def _():
                    sending(t * STEP + j).wait_recv()
                    passing(t * STEP + j).start()

        @pl.when((t >= LATER) & (t < STEPS + LATER))
        def _():
            g = t - LATER
            for j in range(STEP):

                @pl.when(g * STEP + j > 0)
                def _():
                    passed(g * STEP + j).wait_recv()

            experts(g)
            for j in range(STEP):

                @pl.when(g * STEP + j > 0)
                def _():
                    directing(g * STEP + j).start()
            pairing(g).start()

        @pl.when(t >= LAST)
        def _():
            g = t - LAST
            pairing(g).wait_recv()
            these = pl.ds(g * STEP, STEP)
            summed = part[these, :, pl.ds(mine, SHARE)].astype(F32) + part_in[these].astype(F32)
            back[these] = summed.astype(BF16)

            for j in range(STEP):

                @pl.when(g * STEP + j > 0)
                def _():
                    returning(g * STEP + j).start()

    got[0] = back[0]
    got_direct[0] = part[0, :, SHARE:TAKE]

    allowed = (rows_at >= cols_at) & (jnp.concatenate([seg_col[...]] * 2, axis=1) == seg_row)

    def arrived(backward):
        total = jnp.zeros((2, HEAD_DIM, HEAD_DIM), F32)
        for j in range(REACH):
            k = backward * REACH + j
            stating(k).wait_recv()
            if backward:
                same = ends_in[k, 0:1, :] == ends[8:9, :]
                inside = jnp.where(me + 1 + j < OWNERS, 1.0, 0.0)
            else:
                same = ends_in[k, 8:9, :] == ends[0:1, :]
                inside = jnp.where(me - 1 - j >= 0, 1.0, 0.0)
            weight = jnp.where(same, 1.0, 0.0) * inside
            total += state_in[k].astype(F32) * weight[None]
        return total.astype(BF16)

    for j in range(2 * REACH):
        telling(j).wait_recv()
    carried[...] = arrived(0)
    for h in range(2):
        head = slice(h * HEAD_DIM, (h + 1) * HEAD_DIM)
        scores[h] = jnp.where(allowed, dot(q_ref[:, head], k_ref[:, head], ((1,), (1,))), 0.0).astype(BF16)

    y_acc[...] = jnp.zeros_like(y_acc)

    def spreading(b, to):
        return remote(y_out.at[b], y_in.at[z], y_s.at[b], y_r.at[z], me, to)

    def spread(i):
        return remote(y_out.at[0], y_in.at[i], y_s.at[0], y_r.at[i], me, z)

    def out_of(b, to):
        @pl.when(to != z)
        def _():
            spreading(b, to).start()

        @pl.when(to == z)
        def _():
            y_acc[...] = y_sum[:, b * SPAN : (b + 1) * SPAN]

    y_sum[...] = jnp.zeros_like(y_sum)

    @pl.loop(0, STEPS)
    def _(g):
        for j in range(STEP):

            @pl.when(g * STEP + j > 0)
            def _():
                directing(g * STEP + j).wait_recv()

        rows = got_direct[pl.ds(g * STEP, STEP)].reshape(ROWS, TAKE - SHARE)
        y_sum[:, 0 : TAKE - SHARE] += dot(seats(g, False), rows, ((0,), (0,)))

    for b in range(DIRECT):
        y_out[b] = y_sum[:, b * SPAN : (b + 1) * SPAN].astype(BF16)
        out_of(b, LAID[OWN + b])

    for n in range(WIDTH // 256):
        columns = slice(n * 256, (n + 1) * 256)
        down[:, columns] = dot(
            hidden[...], cot[:, :, columns].reshape(OWNERS * SLOTS, 256), ((0,), (0,))
        )
    writing = pltpu.make_async_copy(down, down_out.at[0], down_s)
    writing.start()

    @pl.loop(0, STEPS)
    def _(g):
        for j in range(STEP):

            @pl.when(g * STEP + j > 0)
            def _():
                returning(g * STEP + j).wait_recv()

        rows = got[pl.ds(g * STEP, STEP)].reshape(ROWS, SHARE)
        y_sum[:, TAKE - SHARE : TAKE] += dot(seats(g, False), rows, ((0,), (0,)))

    for b in range(OWN):
        y_out[DIRECT + b] = y_sum[:, (DIRECT + b) * SPAN : (DIRECT + b + 1) * SPAN].astype(BF16)
        even, odd = LAID[b], LAID[OWN + DIRECT + b]
        out_of(DIRECT + b, even + half * (odd - even))

    is_direct = (z == LAID[OWN]) | (z == LAID[OWN + 1])
    odd_own = (z == LAID[5]) | (z == LAID[6]) | (z == LAID[7])
    for i in range(GROUPS):
        wanted = is_direct | odd_own if i % 2 else jnp.logical_not(odd_own)

        @pl.when((z != i) & wanted)
        def _():
            spread(i).wait_recv()
            y_acc[...] += y_in[i].astype(F32)

    for h in range(2):
        head = slice(h * HEAD_DIM, (h + 1) * HEAD_DIM)
        opened = jnp.where(first_mask, q_ref[:, head].astype(F32), 0.0).astype(BF16)
        state_out[1, h] = dot(opened, y_acc[:, head].astype(BF16), ((0,), (0,))).astype(BF16)
    for j in range(REACH, 2 * REACH):
        stating(j).start()

    inner = []
    for h in range(2):
        head = slice(h * HEAD_DIM, (h + 1) * HEAD_DIM)
        g_h = y_acc[:, head].astype(BF16)
        cot_value = jnp.where(allowed, dot(g_h, v_ref[:, head], ((1,), (1,))), 0.0).astype(BF16)
        query_grad = dot(cot_value, k_ref[:, head], ((1,), (0,)))
        query_grad += jnp.where(first_mask, dot(g_h, carried[h], ((1,), (1,))), 0.0)
        small_out[0, :, head] = query_grad.astype(BF16)
        inner.append((dot(cot_value, q_ref[:, head], ((0,), (0,))), dot(scores[h], g_h, ((0,), (0,)))))

    back_state = arrived(1)
    for h in range(2):
        head = slice(h * HEAD_DIM, (h + 1) * HEAD_DIM)
        key_grad, value_grad = inner[h]
        key_part = dot(v_ref[:, head], back_state[h], ((1,), (1,)))
        value_part = dot(k_ref[:, head], back_state[h], ((1,), (0,)))
        small_out[1, :, head] = (key_grad + jnp.where(last_mask, key_part, 0.0)).astype(BF16)
        small_out[2, :, head] = (value_grad + jnp.where(last_mask, value_part, 0.0)).astype(BF16)

    writing.wait()

    @pl.loop(0, STEPS)
    def _(g):
        pairing(g).wait_send()

    @pl.loop(1, OWNERS)
    def _(i):
        sending(i).wait_send()
        passing(i).wait_send()
        returning(i).wait_send()
        directing(i).wait_send()

    for b in range(DIRECT + OWN):
        if b < DIRECT:
            to = LAID[OWN + b]
        else:
            to = LAID[b - DIRECT] + half * (LAID[OWN + b] - LAID[b - DIRECT])

        @pl.when(to != z)
        def _():
            spreading(b, to).wait_send()

    for j in range(2 * REACH):
        telling(j).wait_send()
        stating(j).wait_send()


def hand_over(grads, down_grad, q_out, k_out, v_out, down_out, small, large, come, go):
    count = HIDDEN // PIECE
    pieces = [pl.ds(i * PIECE, PIECE) for i in range(count)]
    chain = [(down_grad.at[0, p], large.at[p], down_out.at[0, p]) for p in pieces]
    chain += [(grads.at[i], small.at[i], out) for i, out in enumerate((q_out, k_out, v_out))]
    into = [pltpu.make_async_copy(a, b, come.at[i]) for i, (a, b, _) in enumerate(chain)]
    out_of = [pltpu.make_async_copy(b, c, go.at[i]) for i, (_, b, c) in enumerate(chain)]
    for copy in into:
        copy.start()
    for first, then in zip(into, out_of):
        first.wait()
        then.start()
    for copy in out_of:
        copy.wait()


def local(
    out_grad, gate_values, expert_ids, segment_ids, gate_pre, up_pre, w_gate, w_up, w_down, queries, keys, values
):
    vmem, hbm = pl.BlockSpec(memory_space=pltpu.VMEM), pl.BlockSpec(memory_space=pl.ANY)
    dma = pltpu.SemaphoreType.DMA
    small = jax.ShapeDtypeStruct((3, TOKENS, SPAN), BF16)
    down = jax.ShapeDtypeStruct((1, HIDDEN, WIDTH), F32)
    states = (2, HEAD_DIM, HEAD_DIM)
    grads, down_grad = pl.pallas_call(
        kernel,
        out_shape=(small, down),
        in_specs=[vmem] * 12,
        out_specs=(vmem, hbm),
        scratch_shapes=[
            pltpu.VMEM((HIDDEN, WIDTH), F32),
            dma,
            pltpu.VMEM((OWNERS, TOKENS), F32),
            pltpu.VMEM((OWNERS, TOKENS), F32),
            pltpu.VMEM((16, 128), F32),
            pltpu.VMEM((TOKENS, 128), F32),
            pltpu.VMEM((OWNERS, SLOTS, GIVE), BF16),
            pltpu.VMEM((OWNERS, SLOTS, WIDTH), BF16),
            pltpu.VMEM((OWNERS, SLOTS, WIDTH), BF16),
            pltpu.VMEM((OWNERS, SLOTS, SHARE), BF16),
            pltpu.VMEM((OWNERS, SLOTS, SHARE), BF16),
            pltpu.VMEM((OWNERS, SLOTS, SHARE), BF16),
            pltpu.VMEM((OWNERS, SLOTS, TAKE - SHARE), BF16),
            pltpu.VMEM((OWNERS * SLOTS, HIDDEN), BF16),
            pltpu.VMEM((TOKENS, TAKE), F32),
            pltpu.VMEM((DIRECT + OWN, TOKENS, SPAN), BF16),
            pltpu.VMEM((GROUPS, TOKENS, SPAN), BF16),
            pltpu.VMEM((TOKENS, SPAN), F32),
            pltpu.VMEM((2, *states), BF16),
            pltpu.VMEM((2 * REACH, *states), BF16),
            pltpu.VMEM((2 * REACH, 16, 128), F32),
            pltpu.VMEM((2, TOKENS, TOKENS), BF16),
            pltpu.VMEM(states, BF16),
            *[dma((OWNERS,))] * 10,
            dma((DIRECT + OWN,)), dma((GROUPS,)), *[dma((2 * REACH,))] * 4,
        ],
        compiler_params=pltpu.CompilerParams(
            collective_id=0, has_side_effects=True, vmem_limit_bytes=58 << 20
        ),
    )(
        expert_ids.T, gate_values.T, segment_ids[None, :], out_grad, gate_pre, up_pre, w_gate, w_up, w_down,
        queries, keys, values,
    )
    one = jax.ShapeDtypeStruct((TOKENS, SPAN), BF16)
    return pl.pallas_call(
        hand_over,
        out_shape=(one, one, one, down),
        in_specs=[hbm, hbm],
        out_specs=(hbm,) * 4,
        scratch_shapes=[
            pltpu.VMEM((3, TOKENS, SPAN), BF16),
            pltpu.VMEM((HIDDEN, WIDTH), F32),
            dma((HIDDEN // PIECE + 3,)),
            dma((HIDDEN // PIECE + 3,)),
        ],
        compiler_params=pltpu.CompilerParams(vmem_limit_bytes=60 << 20),
    )(grads, down_grad)


def solution(mesh):
    row, col = P("ctx", None), P("ctx", "ep")
    both = ("ctx", "ep")
    pre, weight = P(both, None, None, None), P(both, None, None)
    return jax.shard_map(
        local,
        mesh=mesh,
        in_specs=(row, row, row, P("ctx"), pre, pre, weight, weight, weight, col, col, col),
        out_specs=(col, col, col, weight),
        check_vma=False,
    )
```
